32 devices in a mesh: ctx: 16 (over z, x, core), exp: 2 (over y).
Axes of the slice: x: 2, y: 2, z: 4, core: 2. Of those that a mesh axis runs over, the one named last changes fastest.
Arguments:
- feature_in: bfloat16 [6144, 4096], P('ctx', 'exp'), may hold values from -6 to 6
- grad_out: bfloat16 [6144, 4096], P('ctx', 'exp'), may hold values from -6 to 6
- delta: float32 [64, 6144], P('exp', 'ctx'), may hold values from 0.5 to 2
- decay_log: float32 [64], P('exp'), may hold values from -13 to -2
- skip_gain: float32 [64], P('exp'), may hold values from 0.5 to 1.5
- b_proj: float32 [6144, 128], P('ctx'), may hold values from -0.0625 to 0.0625
- c_proj: float32 [6144, 128], P('ctx'), may hold values from -6 to 6
- route_ids: int32 [6144, 4], P('ctx'), may hold values from 0 to 7, all different within a row; in each aligned block of 384 rows (0 to 383, 384 to 767, ...) at most 240 rows name the same one
- route_probs: float32 [6144, 4], P('ctx'), may hold values from 0.05 to 0.5
- w_down: bfloat16 [8, 384, 4096], P('exp'), may hold values from -0.3125 to 0.3125
- saved_act: bfloat16 [16, 8, 240, 384], P('ctx', 'exp'), may hold values from -0.75 to 0.75
Outputs:
- grad_x: bfloat16 [6144, 4096], P('ctx', 'exp')
- grad_delta: float32 [64, 6144], P('exp', 'ctx')
- grad_b: float32 [6144, 128], P(('ctx', 'exp'))
- grad_c: float32 [6144, 128], P(('ctx', 'exp'))
- grad_act: bfloat16 [16, 8, 240, 384], P('ctx', 'exp')
- grad_slots: float32 [16, 8, 240], P('ctx', 'exp')
The draws below stay inside these ranges and needn't reach their ends.
Inputs may be any that keep to these rules, and one draw needn't show every extreme that they name: `route_ids`: each row names 4 different experts; among the rows of one context shard no expert is named more than 240 times, a bound that some block reaches.
All inputs are finite; a program needn't handle non-finite values.
Results may differ from the reference program's by a relative error of at most 0.0049.
Values may be sent and summed in bfloat16 or wider, within the bound.
A program may use at most 256 MiB of HBM per device.

```python
import math
from functools import partial
import jax
import jax.numpy as jnp
import numpy as np
from jax import lax

HEADS = 64
HEAD_DIM = 64
NSTATE = 128
D = 4096
FF = 384
EXPERTS = 8
TOPK = 4
GROUP = 128
SEQ_DEV = 384
SEQ = 6144
CAP = 240
N_CTX = 16


def draw_decay_log(key, part):
    key_pick, key_slow, key_fast = jax.random.split(jax.random.fold_in(key, 11), 3)
    slow_share = 0.5
    chosen = jax.random.uniform(key_pick, (HEADS,), jnp.float32) < slow_share
    slow_rate = jax.random.uniform(key_slow, (HEADS,), jnp.float32, math.log(0.2 / SEQ), math.log(1.5 / SEQ))
    fast_rate = jax.random.uniform(key_fast, (HEADS,), jnp.float32, math.log(1.0 / 60.0), math.log(1.0 / 20.0))
    return jnp.where(chosen, slow_rate, fast_rate).astype(jnp.float32)


def block_levels(stream_key, dims, shards, low, largest):
    def one(dim, shards_of):
        heights = jax.random.uniform(jax.random.fold_in(jax.random.fold_in(stream_key, 6), dim), (shards_of,), jnp.float32, low / len(shards), largest / len(shards))
        return jnp.repeat(jnp.exp(heights), dims[dim] // shards_of).reshape((-1,) + (1,) * (len(dims) - dim - 1))

    level = one(*shards[0])
    for cut in shards[1:]:
        level = level * one(*cut)
    return level


def routed_block(stream_key, own, number, rows, number_of, top, bound, slope):
    sequence = jax.random.permutation(stream_key, number_of)
    crowded, usual = load_shares(number_of, rows * top, bound, slope, True), load_shares(number_of, rows * top, bound, slope, False)
    places = jnp.arange(number_of)

    def named(lengths, rotation):
        used = int((lengths > 0).sum())
        fixed = max(1, used // 4)
        shifted = fixed + (places - fixed + rotation * (used - fixed)) % max(1, number_of - fixed)
        return jnp.zeros((number_of,), jnp.int32).at[sequence[jnp.where(places < fixed, places, shifted)]].set(jnp.asarray(lengths, jnp.int32))

    lengths = jnp.where(number % 4 == 0, named(crowded, number // 4), named(usual, number - number // 4 - 1))
    mixed = jax.random.permutation(jax.random.fold_in(own, 3), number_of)
    giver, taker = mixed[0:number_of // 2 * 2:2], mixed[1:number_of // 2 * 2:2]
    margin = jnp.minimum(lengths[giver] - 1, bound - lengths[taker]) // 2
    margin = jnp.where((giver == sequence[0]) | (taker == sequence[0]) | (lengths[taker] == 0), 0, jnp.maximum(margin, 0))
    shifted = jax.random.randint(jax.random.fold_in(own, 4), (number_of // 2,), 0, 1 << 20) % (margin + 1)
    lengths = lengths.at[giver].add(-shifted).at[taker].add(shifted)
    items = jnp.searchsorted(jnp.cumsum(lengths), jnp.arange(rows * top), side="right").astype(jnp.int32)
    table = items.reshape(top, rows).T
    table = table[jax.random.permutation(jax.random.fold_in(own, 1), rows)]
    rotation = jax.random.randint(jax.random.fold_in(own, 2), (rows, 1), 0, top)
    return jnp.take_along_axis(table, (jnp.arange(top)[None, :] + rotation) % top, axis=1)


def load_shares(count, total, reach, skew, full):
    portions = [(1 << 20) // math.isqrt(rank ** skew) + 1 for rank in range(1, count + 1)]
    largest = reach if full else min(reach, max(-(-total // count), total * portions[0] // sum(portions)))
    least = 1 if total - largest >= count - 1 else 0
    holding, rest = [largest] + [least] * (count - 1), total - largest - least * (count - 1)
    while rest > 0:
        free = [i for i in range(1, count) if holding[i] < largest] or [i for i in range(1, count) if holding[i] < reach]
        mass, budget = sum([portions[i] for i in free]), rest
        for i in free:
            extra = min(reach - holding[i], max(1, budget * portions[i] // mass), rest)
            holding[i] = holding[i] + extra
            rest = rest - extra
    return np.array(holding)


def gaussian(stream_key, dims, scale, bound, cuts=(), held_as=jnp.bfloat16):
    entries = jax.random.normal(stream_key, dims, jnp.float32) * scale
    if len(cuts) > 0:
        entries = block_levels(stream_key, dims, cuts, -0.22, 0.18) * entries
    return jnp.clip(entries, min=-bound, max=bound).astype(held_as)


def setup_inputs(seed: int = 0) -> dict:
    key_list = jax.random.split(jax.random.key(seed), 12)
    feature_in = gaussian(key_list[0], (SEQ, D), 1.0, 6.0, ((0, 16), (1, 2)))
    grad_out = gaussian(key_list[1], (SEQ, D), 1.0, 6.0, ((0, 16), (1, 2)))
    delta = jnp.clip(0.5 + 1.5 * jax.random.uniform(key_list[2], (HEADS, SEQ), jnp.float32) ** block_levels(key_list[2], (HEADS, SEQ), ((0, 2), (1, 16)), -0.2, 0.2), 0.5, 2.0)
    decay_log = draw_decay_log(jax.random.fold_in(key_list[11], 71), 0)
    skip_gain = jnp.clip(0.5 + 1.0 * jax.random.uniform(key_list[4], (HEADS,), jnp.float32) ** block_levels(key_list[4], (HEADS,), ((0, 2),), -0.2, 0.2), 0.5, 1.5)
    b_proj = gaussian(key_list[5], (SEQ, NSTATE), 0.004, 0.0625, ((0, 16),), jnp.float32)
    c_proj = gaussian(key_list[6], (SEQ, NSTATE), 1.0, 6.0, ((0, 16),), jnp.float32)
    route_ids_keys = jax.random.split(jax.random.fold_in(key_list[7], 1), SEQ // SEQ_DEV)
    route_ids_turns = jax.random.permutation(jax.random.fold_in(key_list[7], 3), SEQ // SEQ_DEV)
    route_ids = jax.vmap(lambda own, number: routed_block(jax.random.fold_in(key_list[7], 2), own, number, SEQ_DEV, EXPERTS, TOPK, CAP, 2))(route_ids_keys, route_ids_turns).reshape((SEQ, TOPK))
    route_probs = jnp.clip(0.05 + 0.45 * jax.random.uniform(key_list[8], (SEQ, TOPK), jnp.float32) ** block_levels(key_list[8], (SEQ, TOPK), ((0, 16),), -0.2, 0.2), 0.05, 0.5)
    w_down = gaussian(key_list[9], (EXPERTS, FF, D), FF ** -0.5, 0.3125, ((0, 2),))
    saved_act = gaussian(key_list[10], (N_CTX, EXPERTS, CAP, FF), 0.05, 0.75, ((0, 16), (1, 2)))
    return dict(feature_in=feature_in, grad_out=grad_out, delta=delta, decay_log=decay_log, skip_gain=skip_gain, b_proj=b_proj, c_proj=c_proj, route_ids=route_ids, route_probs=route_probs, w_down=w_down, saved_act=saved_act)


HIGHEST = lax.Precision.HIGHEST

def block_step(neg_rate, skip_gain, carry_state, pieces):
    inputs, deltas, b_block, c_block = pieces
    block_len = inputs.shape[0]
    logdecay = jnp.cumsum(neg_rate[:, None] * deltas, axis=1)
    gram_mat = jnp.dot(c_block, b_block.T, precision=HIGHEST)
    causal = jnp.arange(block_len, dtype=jnp.int32)[:, None] >= jnp.arange(block_len, dtype=jnp.int32)[None, :]
    spread = logdecay[:, :, None] - logdecay[:, None, :]
    weights = jnp.exp(jnp.where(causal[None], spread, -jnp.inf))
    driven = inputs * deltas.T[:, :, None]
    within = jnp.einsum('hts,ts,shp->thp', weights, gram_mat, driven, precision=HIGHEST)
    carried = jnp.einsum('tn,hpn->thp', c_block, carry_state, precision=HIGHEST) * jnp.exp(logdecay).T[:, :, None]
    outputs = within + carried + skip_gain[None, :, None] * inputs
    remain = jnp.exp(logdecay[:, -1:] - logdecay)
    updated = jnp.exp(logdecay[:, -1])[:, None, None] * carry_state + jnp.einsum('sn,shp,hs->hpn', b_block, driven, remain, precision=HIGHEST)
    return (updated, outputs)

def run_blocks(inputs, deltas, b_full, c_full, start_state, neg_rate, skip_gain, block_len, recompute):
    length, head_count, width = inputs.shape
    block_count = length // block_len
    x_blocks = inputs.reshape(block_count, block_len, head_count, width)
    d_blocks = deltas.reshape(head_count, block_count, block_len).transpose(1, 0, 2)
    b_blocks = b_full.reshape(block_count, block_len, -1)
    c_blocks = c_full.reshape(block_count, block_len, -1)
    block_fn = partial(block_step, neg_rate, skip_gain)
    if recompute:
        block_fn = jax.checkpoint(block_fn)
    final_state, outputs = lax.scan(block_fn, start_state, (x_blocks, d_blocks, b_blocks, c_blocks))
    return (outputs.reshape(length, head_count, width), final_state)

def slot_tables(route_ids, route_probs, expert_count, capacity):
    row_count, top_count = route_ids.shape
    flat_ids = route_ids.reshape(-1).astype(jnp.int32)
    one_hot = (flat_ids[:, None] == jnp.arange(expert_count, dtype=jnp.int32)[None, :]).astype(jnp.int32)
    before = jnp.cumsum(one_hot, axis=0).astype(jnp.int32) - one_hot
    slot_rank = lax.optimization_barrier(jnp.sum(before * one_hot, axis=1)).astype(jnp.int32)
    position = (flat_ids * capacity + slot_rank).astype(jnp.int32)
    token_row = (jnp.arange(row_count * top_count, dtype=jnp.int32) // top_count).astype(jnp.int32)
    slot_table = jnp.full((expert_count * capacity,), row_count, dtype=jnp.int32).at[position].set(token_row)
    weight = jnp.zeros((expert_count * capacity,), jnp.float32).at[position].set(route_probs.reshape(-1))
    return (slot_table.reshape(expert_count, capacity), weight.reshape(expert_count, capacity))

def expert_grad(picked, weights_down, act_rows, slot_probs):
    out_row = jnp.dot(act_rows, weights_down, preferred_element_type=jnp.float32)
    grad_slot = lax.optimization_barrier(jnp.sum(picked.astype(jnp.float32) * out_row, axis=1))
    scaled = (slot_probs[:, None] * picked.astype(jnp.float32)).astype(jnp.bfloat16)
    grad_rows = jnp.dot(scaled, weights_down.T, preferred_element_type=jnp.float32).astype(jnp.bfloat16)
    return (grad_rows, grad_slot)

def reference(feature_in, grad_out, delta, decay_log, skip_gain, b_proj, c_proj, route_ids, route_probs, w_down, saved_act):
    neg_rate = -jnp.exp(decay_log)
    inputs = feature_in.astype(jnp.float32).reshape(SEQ, HEADS, HEAD_DIM)
    cotangent = grad_out.astype(jnp.float32).reshape(SEQ, HEADS, HEAD_DIM)
    zero_state = jnp.zeros((HEADS, HEAD_DIM, NSTATE), jnp.float32)

    def forward(feats, deltas, b_full, c_full):
        return run_blocks(feats, deltas, b_full, c_full, zero_state, neg_rate, skip_gain, GROUP, True)[0]
    _, pullback = jax.vjp(forward, inputs, delta, b_proj.astype(jnp.float32), c_proj.astype(jnp.float32))
    grad_feat, grad_delta, grad_b, grad_c = pullback(cotangent)
    grad_rows_all = grad_out.reshape(N_CTX, SEQ_DEV, D)
    ids_all = route_ids.reshape(N_CTX, SEQ_DEV, TOPK)
    probs_all = route_probs.reshape(N_CTX, SEQ_DEV, TOPK)

    def one_shard(pieces):
        shard_rows, shard_ids, shard_probs, shard_acts = pieces
        slot_table, slot_probs = slot_tables(shard_ids, shard_probs, EXPERTS, CAP)
        padded = jnp.concatenate([shard_rows, jnp.zeros((1, D), shard_rows.dtype)], axis=0)

        def one_expert(items):
            index_rows, weights_down, act_rows, probs_slot = items
            return expert_grad(padded[index_rows], weights_down, act_rows, probs_slot)
        return lax.map(one_expert, (slot_table, w_down, shard_acts, slot_probs))
    grad_act, grad_slots = lax.map(one_shard, (grad_rows_all, ids_all, probs_all, saved_act))
    return (grad_feat.reshape(SEQ, D).astype(jnp.bfloat16), grad_delta, grad_b, grad_c, grad_act, grad_slots)
```

```python
from functools import partial

import jax
import jax.numpy as jnp
from jax import lax
from jax.experimental import pallas as pl
from jax.experimental.pallas import tpu as pltpu
from jax.sharding import PartitionSpec as P

HEAD_DIM = 64
CHUNK = 128
LANES = 128
PIECE = 256
SENT = 512
TEAM = 4
HOP_LAPS = 3
LAST_LAPS = 3
LOG2E = 1.4426950408889634
F32 = jnp.float32
BF16 = jnp.bfloat16
MESH = pl.DeviceIdType.MESH


def nn(a, b):
    return lax.dot_general(a, b, (((1,), (0,)), ((), ())), preferred_element_type=F32)


def nt(a, b):
    return lax.dot_general(a, b, (((1,), (1,)), ((), ())), preferred_element_type=F32)


def split(value, count):
    parts = []
    for _ in range(count):
        part = value.astype(BF16)
        parts.append(part)
        value = value - part.astype(F32)
    return parts


def fine(dot, a, b):
    a_hi, a_lo = split(a, 2)
    b_hi, b_lo = split(b, 2)
    return dot(a_hi, b_hi) + (dot(a_hi, b_lo) + dot(a_lo, b_hi))


def stacked(value):
    return jnp.concatenate([part.astype(F32) for part in split(value, 3)], axis=0)


def iota(shape, dim):
    return lax.broadcasted_iota(jnp.int32, shape, dim)


def block_kernel(
    n_ctx, n_exp,
    x_any, g_any, delta_any, decay_any, skip_any, b_any, c_any, ids_any, probs_any, act_any, w_any,
    grad_x_ref, grad_delta_ref, grad_b_ref, grad_c_ref, grad_act_ref, grad_slots_ref,
    x_ref, g_ref, delta_ref, decay_ref, skip_ref, b_ref, c_ref, ids_ref, probs_ref, act_ref, w_ref,
    g_in, t_all, t_lanes, factor, plane, skip_x, sel_ref,
    grow_k, keep_k, off_k, log_rows, b_bf, c_bf, b_t_ref, c_t_ref,
    gram_t, dgram_t, row_u, uv_ref, end_ref, part_b, part_c, land_b, land_c,
    chunk_own, own, own_in, pair_sum, z_in, z_out, x_out, x_in, core_out, entry,
    grow_x_ref, keep_x_ref, kept_ref, grown_ref, inside, product, chosen_ref, weight_ref, slot_rows,
    load_sem, load_w, send_g, recv_g, send_t, recv_t, send_c, recv_c, send_z, recv_z,
    send_x, recv_x, send_d, recv_d, send_p, recv_p, send_q, recv_q,
):
    me, side = lax.axis_index("ctx"), lax.axis_index("exp")
    teams = n_ctx // TEAM
    core, column, row = lax.rem(me, 2), lax.rem(me // 2, 2), me // TEAM
    spot = lax.rem(me, TEAM)
    first_member = me - spot
    mate = me + 1 - 2 * core
    across = me + 2 - 4 * column

    arrays = [
        (delta_any, delta_ref), (decay_any, decay_ref), (b_any, b_ref), (c_any, c_ref),
        (x_any, x_ref), (g_any, g_ref), (skip_any, skip_ref), (ids_any, ids_ref),
        (probs_any, probs_ref), (act_any, act_ref),
    ]
    loads = [
        pltpu.make_async_copy(src, dst, load_sem.at[i]) for i, (src, dst) in enumerate(arrays)
    ]
    for load in loads:
        load.start()
    experts = w_ref.shape[0]
    w_loads = [
        pltpu.make_async_copy(w_any.at[e], w_ref.at[e], load_w.at[e]) for e in range(experts)
    ]
    for load in w_loads:
        load.start()

    barrier = pltpu.get_barrier_semaphore()

    def greet(ctx, exp):
        pl.semaphore_signal(barrier, inc=1, device_id=(ctx, exp), device_id_type=MESH)

    for k in range(1, n_exp):
        greet(me, lax.rem(side + k, n_exp))
    for k in range(1, TEAM):
        greet(first_member + lax.rem(spot + k, TEAM), side)

    @pl.when(row > 0)
    def _():
        greet(me - TEAM, side)

    @pl.when(row < teams - 1)
    def _():
        greet(me + TEAM, side)

    met = n_exp - 1 + TEAM - 1 + (row > 0).astype(jnp.int32) + (row < teams - 1).astype(jnp.int32)
    pl.semaphore_wait(barrier, met)

    length, width = x_ref.shape
    sent = g_in.shape[3]
    sends = width // sent

    def to_partner(k, p):
        return pltpu.make_async_remote_copy(
            src_ref=g_any.at[:, pl.ds(p * sent, sent)],
            dst_ref=g_in.at[k - 1, p],
            send_sem=send_g.at[k - 1, p],
            recv_sem=recv_g.at[k - 1, p],
            device_id=(me, lax.rem(side + k, n_exp)),
            device_id_type=MESH,
        )

    for p in range(sends):
        for k in range(1, n_exp):
            to_partner(k, p).start()

    heads = delta_ref.shape[0]
    chunks = length // CHUNK
    parts = [slice(c * CHUNK, (c + 1) * CHUNK) for c in range(chunks)]
    pieces = width // PIECE
    per = LANES // HEAD_DIM
    held = PIECE // HEAD_DIM
    nstate = b_ref.shape[1]
    half = nstate // 2
    my_rows = pl.ds(pl.multiple_of(core * half, half), half)
    mate_rows = pl.ds(pl.multiple_of((1 - core) * half, half), half)

    def piece_lanes(p):
        return pl.ds(pl.multiple_of(p * PIECE, PIECE), PIECE)

    loads[0].wait()
    loads[1].wait()
    delta = delta_ref[...]
    rate_row = -jnp.exp(decay_ref[...])
    same = iota((heads, heads), 0) == iota((heads, heads), 1)
    rate = jnp.sum(jnp.where(same, rate_row, 0.0), axis=1, keepdims=True)
    upper = (iota((CHUNK, CHUNK), 0) <= iota((CHUNK, CHUNK), 1)).astype(BF16)
    pace = delta * rate
    rows = jnp.concatenate([pace[:, part] for part in parts], axis=0)
    sums = None
    for piece in split(rows, 3):
        term = nn(piece, upper)
        sums = term if sums is None else sums + term
    total = None
    for c in range(chunks):
        part = parts[c]
        log = sums[c * heads : (c + 1) * heads]
        end = log[:, CHUNK - 1 : CHUNK]
        total = end if total is None else total + end
        step = delta[:, part]
        grow_k[c] = stacked(jnp.exp(log)).T.astype(BF16)
        keep_k[c] = stacked(jnp.exp(end - log) * step).T.astype(BF16)
        off_k[c] = stacked((jnp.log(step) - log) * LOG2E).T.astype(BF16)
        log = log * LOG2E
        for i in range(width // LANES):
            log_rows[i, :, part] = log[i * per : (i + 1) * per]
    through_row = jnp.sum(jnp.where(same, jnp.exp(total), 0.0), axis=0, keepdims=True)
    t_all[0] = jnp.broadcast_to(
        jnp.concatenate([through_row, jnp.zeros((1, LANES - heads), F32)], axis=1), (8, LANES)
    )

    def tell(k):
        return pltpu.make_async_remote_copy(
            src_ref=t_all.at[0],
            dst_ref=t_all.at[k],
            send_sem=send_t.at[k - 1],
            recv_sem=recv_t.at[k - 1],
            device_id=(first_member + lax.rem(spot + k, TEAM), side),
            device_id_type=MESH,
        )

    for k in range(1, TEAM):
        tell(k).start()

    stack_row = iota((3 * heads, PIECE), 0)
    stack_head = lax.rem(stack_row, heads)

    @pl.loop(0, pieces)
    def _(p):
        sel_ref[p] = (stack_head == p * held + iota((3 * heads, PIECE), 1) // HEAD_DIM).astype(BF16)

    loads[2].wait()
    loads[3].wait()
    b_bf[...] = b_ref[...].astype(BF16)
    c_bf[...] = c_ref[...].astype(BF16)
    b_t_ref[...] = b_ref[...].T.astype(BF16)
    c_t_ref[...] = c_ref[...].T.astype(BF16)
    loads[4].wait()
    loads[5].wait()

    def core_swap(d, k):
        return pltpu.make_async_remote_copy(
            src_ref=own.at[d, k, mate_rows],
            dst_ref=own_in.at[d, k],
            send_sem=send_c.at[d, k],
            recv_sem=recv_c.at[d, k],
            device_id=(mate, side),
            device_id_type=MESH,
        )

    def along(d, k):
        return pltpu.make_async_remote_copy(
            src_ref=z_out.at[d, k],
            dst_ref=z_in.at[d, k],
            send_sem=send_z.at[d, k],
            recv_sem=recv_z.at[d, k],
            device_id=(me + TEAM if d == 0 else me - TEAM, side),
            device_id_type=MESH,
        )

    def crossing(d, k):
        return pltpu.make_async_remote_copy(
            src_ref=x_out.at[d, k],
            dst_ref=x_in.at[d, k],
            send_sem=send_x.at[d, k],
            recv_sem=recv_x.at[d, k],
            device_id=(across, side),
            device_id_type=MESH,
        )

    def hand_over(d, k):
        return pltpu.make_async_remote_copy(
            src_ref=core_out.at[d, k],
            dst_ref=entry.at[d, k, my_rows],
            send_sem=send_d.at[d, k],
            recv_sem=recv_d.at[d, k],
            device_id=(mate, side),
            device_id_type=MESH,
        )

    leads = [core == 0, core == 1]
    near = [column == 0, column == 1]
    place = [row, teams - 1 - row]

    def own_unit(p):
        lanes = piece_lanes(p)
        sel = sel_ref[p]
        through, fwd, bwd = [], [], []
        for c in range(chunks):
            part = parts[c]
            grow_x = nn(grow_k[c], sel)
            keep_x = nn(keep_k[c], sel)
            kept = (x_ref[part, lanes].astype(F32) * keep_x).astype(BF16)
            grown = (g_ref[part, lanes].astype(F32) * grow_x).astype(BF16)
            grow_x_ref[part, lanes] = grow_x
            keep_x_ref[part, lanes] = keep_x
            kept_ref[part, lanes] = kept
            grown_ref[part, lanes] = grown
            through.append(grow_x[CHUNK - 1 : CHUNK, :])
            fwd.append(nn(b_t_ref[:, part], kept))
            bwd.append(nn(c_t_ref[:, part], grown))
            chunk_own[0, c, p] = fwd[c]
            chunk_own[1, c, p] = bwd[c]
        total_f, total_b = fwd[0], bwd[chunks - 1]
        for c in range(1, chunks):
            total_f = through[c] * total_f + fwd[c]
        for c in reversed(range(chunks - 1)):
            total_b = through[c] * total_b + bwd[c]
        own[0, p] = total_f
        own[1, p] = total_b
        core_swap(0, p).start()
        core_swap(1, p).start()

    def gather(k, d):
        lanes = piece_lanes(k)
        core_swap(d, k).wait_recv()
        mine, theirs = own[d, k, my_rows], own_in[d, k]
        first = jnp.where(leads[d], mine, theirs)
        second = jnp.where(leads[d], theirs, mine)
        pair_sum[d, k] = factor[d, 1, 0:1, lanes] * first + second

    def pass_on(k, d):
        lanes = piece_lanes(k)

        @pl.when(place[d] == 0)
        def _():
            z_in[d, k] = jnp.zeros((half, PIECE), F32)

        @pl.when(place[d] > 0)
        def _():
            along(d, k).wait_recv()

        before, mine = z_in[d, k], pair_sum[d, k]

        @pl.when(place[d] < teams - 1)
        def _():
            z_out[d, k] = plane[0:1, lanes] * before + factor[d, 2, 0:1, lanes] * mine
            along(d, k).start()

        x_out[d, k] = jnp.where(near[d], factor[d, 3, 0:1, lanes] * before + mine, before).astype(BF16)
        crossing(d, k).start()

    def settle(k, d):
        lanes = piece_lanes(k)
        crossing(d, k).wait_recv()
        before, other = z_in[d, k], x_in[d, k].astype(F32)
        into = jnp.where(near[d], before + other, factor[d, 3, 0:1, lanes] * before + other)
        first = jnp.where(leads[d], own[d, k, my_rows], own_in[d, k])
        after = factor[d, 0, 0:1, lanes] * into + first
        entry[d, k, my_rows] = jnp.where(leads[d], into, after)
        core_out[d, k] = jnp.where(leads[d], after, into)
        hand_over(d, k).start()

    def stage(step, offset, act, d):
        k = step - offset

        @pl.when((k >= 0) & (k < pieces))
        def _():
            act(k, d)

    def exchange(step):
        for d in range(2):
            stage(step, 1, gather, d)
            stage(step, 1 + HOP_LAPS * place[d], pass_on, d)
            stage(step, 1 + HOP_LAPS * place[d] + LAST_LAPS, settle, d)

    own_unit(0)

    for k in range(1, TEAM):
        tell(k).wait_recv()
    loads[6].wait()
    skip_row = jnp.broadcast_to(skip_ref[...], (8, heads))

    def over_lanes(value):
        return jnp.concatenate([part.astype(F32) for part in split(value, 3)], axis=1).astype(BF16)

    spread_rows = [over_lanes(t_all[k][:, :heads]) for k in range(TEAM)] + [over_lanes(skip_row)]
    spread_rows = jnp.concatenate([value.astype(F32) for value in spread_rows], axis=0).astype(BF16)

    @pl.loop(0, pieces)
    def _(p):
        lanes = piece_lanes(p)
        lifted = nn(spread_rows, sel_ref[p])
        for k in range(TEAM):
            t_lanes[k, :, lanes] = lifted[8 * k : 8 * k + 8]
        skip_x[:, lanes] = lifted[8 * TEAM : 8 * TEAM + 8]

    def through_of(member):
        return t_lanes[lax.rem(spot - member + TEAM, TEAM)]

    t0, t1, t2, t3 = [through_of(member) for member in range(TEAM)]
    pair0, pair1 = t0 * t1, t2 * t3
    low, high = jnp.where(column == 0, t0, t2), jnp.where(column == 0, t1, t3)
    plane[...] = pair0 * pair1
    factor[0, 0], factor[0, 1] = low, high
    factor[1, 0], factor[1, 1] = high, low
    factor[0, 2] = jnp.where(near[0], pair1, 1.0)
    factor[1, 2] = jnp.where(near[1], pair0, 1.0)
    factor[0, 3], factor[1, 3] = pair0, pair1

    @pl.loop(1, pieces)
    def _(p):
        own_unit(p)
        exchange(p)

    causal = iota((CHUNK, CHUNK), 1) >= iota((CHUNK, CHUNK), 0)
    for part in parts:
        gram_t[part] = jnp.where(causal, fine(nt, b_ref[part], c_ref[part]), 0.0)
    dgram_t[...] = jnp.zeros_like(dgram_t)
    pairs = width // LANES
    low_lanes = (iota((1, LANES), 1) < HEAD_DIM).astype(BF16)
    high_lanes = (iota((1, LANES), 1) >= HEAD_DIM).astype(BF16)
    wide_head = lax.rem(iota((3 * heads, per * CHUNK), 0), heads)

    def within_unit(i):
        lanes = pl.ds(pl.multiple_of(i * LANES, LANES), LANES)
        picks = (wide_head == i * per + iota((3 * heads, per * CHUNK), 1) // CHUNK).astype(BF16)
        for c in range(chunks):
            part = parts[c]
            g_part = g_ref[part, lanes]
            both = jnp.concatenate([g_part * low_lanes, g_part * high_lanes], axis=0)
            pair = nt(x_ref[part, lanes], both)
            offset = nn(off_k[c], picks)
            gram = gram_t[part]
            weighed = []
            total = None
            for j in range(per):
                columns = slice(j * CHUNK, (j + 1) * CHUNK)
                weight = jnp.exp2(offset[:, columns] + log_rows[i, j : j + 1, part])
                bent = weight * gram
                value = weight * pair[:, columns]
                total = value if total is None else total + value
                row_u[i, j : j + 1, part] = jnp.sum(bent * pair[:, columns], axis=0, keepdims=True)
                weighed.append(bent.astype(BF16))
            dgram_t[part] += total
            inside[part, lanes] = nn(jnp.concatenate(weighed, axis=1), both)

    @pl.loop(0, pairs)
    def _(i):
        within_unit(i)
        exchange(pieces + i)

    for load in loads[7:]:
        load.wait()
    for load in w_loads:
        load.wait()
    capacity = act_ref.shape[1]
    before = (iota((length, length), 0) < iota((length, length), 1)).astype(BF16)

    def own_product(e):
        named = ids_ref[...] == side * experts + e
        hit = jnp.sum(named.astype(F32), axis=0, keepdims=True)
        rank = nn(jnp.broadcast_to(hit, (16, length)).astype(BF16), before)[0:1, :]
        place_row = jnp.where(hit > 0.5, rank, -1.0)
        picked = iota((capacity, length), 0).astype(F32) == place_row
        chosen_ref[e] = picked.astype(BF16)
        prob = jnp.sum(jnp.where(named, probs_ref[...], 0.0), axis=0, keepdims=True)
        weight = jnp.sum(jnp.where(picked, prob, 0.0), axis=1, keepdims=True)
        weight_ref[e] = jnp.broadcast_to(weight, (capacity, LANES))
        columns = pl.ds(pl.multiple_of(side * width, width), width)
        product[e] = nt(g_ref[...], w_ref[e, :, columns])

    @pl.loop(0, experts)
    def _(e):
        own_product(e)
        exchange(pieces + pairs + e)

    laps = pieces + pairs + experts
    needed = pieces + HOP_LAPS * (teams - 1) + LAST_LAPS + 1

    if needed > laps:
        @pl.loop(laps, needed)
        def _(step):
            exchange(step)

    for part in parts:
        pull = jnp.where(causal, dgram_t[part], 0.0)
        part_b[part] = fine(nn, pull, c_ref[part])
        part_c[part] = fine(nn, pull.T, b_ref[part])
    end_ref[...] = jnp.zeros_like(end_ref)
    lane_head = lax.rem(iota((16, 4 * PIECE), 1), PIECE) // HEAD_DIM
    lane_kind = iota((16, 4 * PIECE), 1) // (2 * PIECE)
    gather_rows = (iota((16, 4 * PIECE), 0) == lane_head + held * lane_kind).astype(BF16)

    def across_unit(p):
        lanes = piece_lanes(p)
        hand_over(0, p).wait_recv()
        hand_over(1, p).wait_recv()
        through = [grow_x_ref[(c + 1) * CHUNK - 1 : (c + 1) * CHUNK, lanes] for c in range(chunks)]
        states = [entry[0, p]]
        for c in range(chunks):
            states.append(through[c] * states[c] + chunk_own[0, c, p])
        grads = [None] * chunks + [entry[1, p]]
        for c in reversed(range(1, chunks)):
            grads[c] = through[c] * grads[c + 1] + chunk_own[1, c, p]
        skip = skip_x[0:1, lanes]
        for c in range(chunks):
            part = parts[c]
            state, grad = states[c].astype(BF16), grads[c + 1].astype(BF16)
            x_part, g_part = x_ref[part, lanes].astype(F32), g_ref[part, lanes].astype(F32)
            from_grad = nn(b_bf[part], grad) * keep_x_ref[part, lanes]
            from_state = nn(c_bf[part], state) * grow_x_ref[part, lanes]
            part_c[part] += nt(grown_ref[part, lanes], state)
            part_b[part] += nt(kept_ref[part, lanes], grad)
            inner = inside[part, lanes] + from_grad
            grad_x_ref[part, lanes] = (inner + skip * g_part).astype(BF16)
            end_ref[c : c + 1, lanes] = jnp.sum(states[c + 1] * grads[c + 1], axis=0, keepdims=True)
            summed = split(x_part * inner, 2) + split(g_part * from_state, 2)
            uv_ref[p, :, part] = nt(gather_rows, jnp.concatenate(summed, axis=1))

    @pl.loop(0, pieces)
    def _(p):
        across_unit(p)

    share = grad_b_ref.shape[0]

    def shed(k, source, landing, send, recv):
        target = lax.rem(side + k, n_exp)
        return pltpu.make_async_remote_copy(
            src_ref=source.at[pl.ds(pl.multiple_of(target * share, share), share)],
            dst_ref=landing.at[k - 1],
            send_sem=send.at[k - 1],
            recv_sem=recv.at[k - 1],
            device_id=(me, target),
            device_id_type=MESH,
        )

    for k in range(1, n_exp):
        shed(k, part_b, land_b, send_p, recv_p).start()
        shed(k, part_c, land_c, send_q, recv_q).start()

    endings = None
    for piece in split(end_ref[...], 2):
        term = None
        for p in range(pieces):
            value = nt(piece[:, p * PIECE : (p + 1) * PIECE], sel_ref[p, 0:heads])
            term = value if term is None else term + value
        endings = term if endings is None else endings + term
    endings = endings.T
    v_rows = jnp.concatenate([uv_ref[p, 0:held] for p in range(pieces)], axis=0)
    u_rows = jnp.concatenate([uv_ref[p, held : 2 * held] for p in range(pieces)], axis=0)
    net = jnp.concatenate([row_u[i] for i in range(pairs)], axis=0) + u_rows - v_rows
    lower = (iota((CHUNK, CHUNK), 0) >= iota((CHUNK, CHUNK), 1)).astype(BF16)
    rows = jnp.concatenate([net[:, part] for part in parts], axis=0)
    sums = None
    for piece in split(rows, 3):
        term = nn(piece, lower)
        sums = term if sums is None else sums + term
    for c in range(chunks):
        part = parts[c]
        drift = sums[c * heads : (c + 1) * heads] + endings[:, c : c + 1]
        grad_delta_ref[:, part] = v_rows[:, part] / delta_ref[:, part] + rate * drift

    for k in range(1, n_exp):
        owner = lax.rem(side + n_exp - k, n_exp)
        for p in range(sends):
            to_partner(k, p).wait_recv()
            columns = pl.ds(pl.multiple_of(owner * width + p * sent, sent), sent)

            @pl.loop(0, experts)
            def _(e):
                product[e] += nt(g_in[k - 1, p], w_ref[e, :, columns])

    @pl.loop(0, experts)
    def _(e):
        inner = None
        for piece in split(product[e], 2):
            term = nn(chosen_ref[e], piece)
            inner = term if inner is None else inner + term
        grad_act_ref[e] = (weight_ref[e][:, 0:1] * inner).astype(BF16)
        scored = act_ref[e].astype(F32) * inner
        ones = jnp.ones((16, scored.shape[1]), BF16)
        summed = None
        for piece in split(scored, 2):
            term = nt(ones, piece)
            summed = term if summed is None else summed + term
        slot_rows[e] = summed[0:1, :]

    for e in range(experts):
        grad_slots_ref[e : e + 1, :] = slot_rows[e]
    mine = pl.ds(pl.multiple_of(side * share, share), share)
    total_b, total_c = part_b[mine], part_c[mine]
    for k in range(1, n_exp):
        shed(k, part_b, land_b, send_p, recv_p).wait_recv()
        shed(k, part_c, land_c, send_q, recv_q).wait_recv()
        total_b = total_b + land_b[k - 1]
        total_c = total_c + land_c[k - 1]
    grad_b_ref[...] = total_b
    grad_c_ref[...] = total_c

    for k in range(1, n_exp):
        shed(k, part_b, land_b, send_p, recv_p).wait_send()
        shed(k, part_c, land_c, send_q, recv_q).wait_send()
        for p in range(sends):
            to_partner(k, p).wait_send()
    for k in range(1, TEAM):
        tell(k).wait_send()

    @pl.loop(0, pieces)
    def _(p):
        for d in range(2):
            core_swap(d, p).wait_send()
            crossing(d, p).wait_send()
            hand_over(d, p).wait_send()

            @pl.when(place[d] < teams - 1)
            def _():
                along(d, p).wait_send()


def store_kernel(count, *refs):
    sources, targets, sem = refs[:count], refs[count : 2 * count], refs[2 * count]
    copies = [pltpu.make_async_copy(sources[i], targets[i], sem.at[i]) for i in range(count)]
    for copy in copies:
        copy.start()
    for copy in copies:
        copy.wait()


def per_device(
    n_ctx, n_exp,
    feature_in, grad_out, delta, decay_log, skip_gain, b_proj, c_proj,
    route_ids, route_probs, w_down, saved_act,
):
    length, width = feature_in.shape
    heads = delta.shape[0]
    nstate = b_proj.shape[1]
    experts, hidden, full = w_down.shape
    capacity = saved_act.shape[2]
    topk = route_ids.shape[1]
    share = length // n_exp
    others = n_exp - 1
    chunks = length // CHUNK
    pieces = width // PIECE
    half = nstate // 2
    sent = min(SENT, width)
    sends = width // sent
    vmem = pl.BlockSpec(memory_space=pltpu.VMEM)
    hbm = pl.BlockSpec(memory_space=pltpu.HBM)
    dma = pltpu.SemaphoreType.DMA
    inputs = (
        feature_in, grad_out, delta, decay_log[None, :], skip_gain[None, :], b_proj, c_proj,
        route_ids.T, route_probs.T, saved_act[0], w_down,
    )
    shard = jax.ShapeDtypeStruct((share, nstate), F32)
    shapes = (
        jax.ShapeDtypeStruct((length, width), BF16),
        jax.ShapeDtypeStruct((heads, length), F32),
        shard,
        shard,
        jax.ShapeDtypeStruct((experts, capacity, hidden), BF16),
        jax.ShapeDtypeStruct((experts, capacity), F32),
    )
    by_state = pltpu.VMEM((length, nstate), F32)
    per = LANES // HEAD_DIM
    by_pair = pltpu.VMEM((heads // per, per, length), F32)
    wide = pltpu.VMEM((length, width), F32)
    narrow = pltpu.VMEM((length, width), BF16)
    halves = pltpu.VMEM((2, pieces, half, PIECE), F32)
    halves_bf = pltpu.VMEM((2, pieces, half, PIECE), BF16)
    whole = pltpu.VMEM((2, pieces, nstate, PIECE), F32)
    results = pl.pallas_call(
        partial(block_kernel, n_ctx, n_exp),
        out_shape=shapes,
        in_specs=[hbm] * len(inputs),
        out_specs=(vmem,) * len(shapes),
        scratch_shapes=[pltpu.VMEM(value.shape, value.dtype) for value in inputs]
        + [
            pltpu.VMEM((others, sends, length, sent), BF16),
            pltpu.VMEM((TEAM, 8, LANES), F32),
            pltpu.VMEM((TEAM, 8, width), F32),
            pltpu.VMEM((2, 4, 8, width), F32),
            pltpu.VMEM((8, width), F32),
            pltpu.VMEM((8, width), F32),
            pltpu.VMEM((pieces, 3 * heads, PIECE), BF16),
        ]
        + [pltpu.VMEM((chunks, CHUNK, 3 * heads), BF16)] * 3
        + [by_pair]
        + [pltpu.VMEM((length, nstate), BF16)] * 2
        + [pltpu.VMEM((nstate, length), BF16)] * 2
        + [pltpu.VMEM((length, CHUNK), F32)] * 2
        + [by_pair]
        + [pltpu.VMEM((pieces, 16, length), F32), pltpu.VMEM((8, width), F32)]
        + [by_state] * 2
        + [pltpu.VMEM((others, share, nstate), F32)] * 2
        + [pltpu.VMEM((2, chunks, pieces, nstate, PIECE), F32)]
        + [whole]
        + [halves] * 4
        + [halves_bf] * 2
        + [halves, whole]
        + [wide] * 2
        + [narrow] * 2
        + [wide]
        + [
            pltpu.VMEM((experts, length, hidden), F32),
            pltpu.VMEM((experts, capacity, length), BF16),
            pltpu.VMEM((experts, capacity, LANES), F32),
            pltpu.VMEM((experts, 1, capacity), F32),
        ]
        + [dma((10,)), dma((experts,))]
        + [dma((others, sends))] * 2
        + [dma((TEAM - 1,))] * 2
        + [dma((2, pieces))] * 8
        + [dma((others,))] * 4,
        compiler_params=pltpu.CompilerParams(
            collective_id=0, has_side_effects=True, vmem_limit_bytes=58 << 20
        ),
        name="block_grads",
    )(*inputs)
    grad_x, grad_delta, grad_b, grad_c, grad_act, grad_slots = pl.pallas_call(
        partial(store_kernel, len(shapes)),
        out_shape=shapes,
        in_specs=[vmem] * len(shapes),
        out_specs=(hbm,) * len(shapes),
        scratch_shapes=[dma((len(shapes),))],
        name="store",
    )(*results)
    return (grad_x, grad_delta, grad_b, grad_c, grad_act[None], grad_slots[None])


def solution(mesh):
    placed = (
        P("ctx", "exp"),
        P("ctx", "exp"),
        P("exp", "ctx"),
        P("exp"),
        P("exp"),
        P("ctx", None),
        P("ctx", None),
        P("ctx", None),
        P("ctx", None),
        P("exp", None, None),
        P("ctx", "exp", None, None),
    )
    return jax.shard_map(
        partial(per_device, mesh.shape["ctx"], mesh.shape["exp"]),
        mesh=mesh,
        in_specs=placed,
        out_specs=(
            P("ctx", "exp"),
            P("exp", "ctx"),
            P(("ctx", "exp"), None),
            P(("ctx", "exp"), None),
            P("ctx", "exp", None, None),
            P("ctx", "exp", None),
        ),
        check_vma=False,
    )
```

```python
from functools import partial

import jax
import jax.numpy as jnp
from jax import lax
from jax.experimental import pallas as pl
from jax.experimental.pallas import tpu as pltpu
from jax.sharding import PartitionSpec as P

HEAD_DIM = 64
CHUNK = 128
LANES = 128
PIECE = 256
SENT = 512
TEAM = 4
STORE_CUTS = 4
HOP_LAPS = 5
LAST_LAPS = 4
LOG2E = 1.4426950408889634
F32 = jnp.float32
BF16 = jnp.bfloat16
MESH = pl.DeviceIdType.MESH


def nn(a, b):
    return lax.dot_general(a, b, (((1,), (0,)), ((), ())), preferred_element_type=F32)


def nt(a, b):
    return lax.dot_general(a, b, (((1,), (1,)), ((), ())), preferred_element_type=F32)


def split(value, count):
    parts = []
    for _ in range(count):
        part = value.astype(BF16)
        parts.append(part)
        value = value - part.astype(F32)
    return parts


def fine(dot, a, b):
    a_hi, a_lo = split(a, 2)
    b_hi, b_lo = split(b, 2)
    return dot(a_hi, b_hi) + (dot(a_hi, b_lo) + dot(a_lo, b_hi))


def stacked(value):
    return jnp.concatenate([part.astype(F32) for part in split(value, 3)], axis=0)


def iota(shape, dim):
    return lax.broadcasted_iota(jnp.int32, shape, dim)


def block_kernel(
    n_ctx, n_exp,
    x_any, g_any, delta_any, decay_any, skip_any, b_any, c_any, ids_any, probs_any, act_any, w_any,
    grad_x_any, grad_delta_any, grad_b_any, grad_c_any, grad_act_any, grad_slots_any,
    grad_x_ref, grad_delta_ref, grad_b_ref, grad_c_ref, grad_act_ref, grad_slots_ref,
    x_ref, g_ref, delta_ref, decay_ref, skip_ref, b_ref, c_ref, ids_ref, probs_ref, act_ref, w_ref,
    g_in, t_all, t_lanes, factor, plane, skip_x, sel_ref,
    grow_k, keep_k, off_k, log_rows, b_bf, c_bf, b_t_ref, c_t_ref,
    gram_t, dgram_t, row_u, uv_ref, end_ref, part_b, part_c, land_b, land_c,
    chunk_own, own, own_in, pair_sum, z_in, z_out, x_out, x_in, core_out, entry,
    grow_x_ref, keep_x_ref, kept_ref, grown_ref, inside, product, chosen_ref, weight_ref,
    load_sem, load_w, save_x, save_act, save_sem, send_g, recv_g, send_t, recv_t, send_c, recv_c, send_z, recv_z,
    send_x, recv_x, send_d, recv_d, send_p, recv_p, send_q, recv_q,
):
    me, side = lax.axis_index("ctx"), lax.axis_index("exp")
    teams = n_ctx // TEAM
    core, column, row = lax.rem(me, 2), lax.rem(me // 2, 2), me // TEAM
    spot = lax.rem(me, TEAM)
    first_member = me - spot
    mate = me + 1 - 2 * core
    across = me + 2 - 4 * column

    arrays = [
        (delta_any, delta_ref), (decay_any, decay_ref), (b_any, b_ref), (c_any, c_ref),
        (x_any, x_ref), (g_any, g_ref), (skip_any, skip_ref), (ids_any, ids_ref),
        (probs_any, probs_ref), (act_any, act_ref),
    ]
    loads = [
        pltpu.make_async_copy(src, dst, load_sem.at[i]) for i, (src, dst) in enumerate(arrays)
    ]
    for load in loads:
        load.start()
    experts, hidden = w_any.shape[0], w_any.shape[1]
    width = x_ref.shape[1]

    def w_load(e, owner):
        columns = pl.ds(pl.multiple_of(owner * width, width), width)
        return pltpu.make_async_copy(
            w_any.at[e, :, columns], w_ref.at[pl.ds(e * hidden, hidden)], load_w.at[e]
        )

    for e in range(experts):
        w_load(e, side).start()

    barrier = pltpu.get_barrier_semaphore()

    def greet(ctx, exp):
        pl.semaphore_signal(barrier, inc=1, device_id=(ctx, exp), device_id_type=MESH)

    for k in range(1, n_exp):
        greet(me, lax.rem(side + k, n_exp))
    for k in range(1, TEAM):
        greet(first_member + lax.rem(spot + k, TEAM), side)

    @pl.when(row > 0)
    def _():
        greet(me - TEAM, side)

    @pl.when(row < teams - 1)
    def _():
        greet(me + TEAM, side)

    met = n_exp - 1 + TEAM - 1 + (row > 0).astype(jnp.int32) + (row < teams - 1).astype(jnp.int32)
    pl.semaphore_wait(barrier, met)

    length = x_ref.shape[0]
    sent = g_in.shape[3]
    sends = width // sent

    def to_partner(k, p):
        return pltpu.make_async_remote_copy(
            src_ref=g_any.at[:, pl.ds(p * sent, sent)],
            dst_ref=g_in.at[k - 1, p],
            send_sem=send_g.at[k - 1, p],
            recv_sem=recv_g.at[k - 1, p],
            device_id=(me, lax.rem(side + k, n_exp)),
            device_id_type=MESH,
        )

    for p in range(sends):
        for k in range(1, n_exp):
            to_partner(k, p).start()

    heads = delta_ref.shape[0]
    chunks = length // CHUNK
    parts = [slice(c * CHUNK, (c + 1) * CHUNK) for c in range(chunks)]
    pieces = width // PIECE
    per = LANES // HEAD_DIM
    held = PIECE // HEAD_DIM
    nstate = b_ref.shape[1]
    half = nstate // 2
    my_rows = pl.ds(pl.multiple_of(core * half, half), half)
    mate_rows = pl.ds(pl.multiple_of((1 - core) * half, half), half)

    def piece_lanes(p):
        return pl.ds(pl.multiple_of(p * PIECE, PIECE), PIECE)

    loads[0].wait()
    loads[1].wait()
    delta = delta_ref[...]
    rate_row = -jnp.exp(decay_ref[...])
    same = iota((heads, heads), 0) == iota((heads, heads), 1)
    rate = jnp.sum(jnp.where(same, rate_row, 0.0), axis=1, keepdims=True)
    upper = (iota((CHUNK, CHUNK), 0) <= iota((CHUNK, CHUNK), 1)).astype(BF16)
    pace = delta * rate
    rows = jnp.concatenate([pace[:, part] for part in parts], axis=0)
    sums = None
    for piece in split(rows, 3):
        term = nn(piece, upper)
        sums = term if sums is None else sums + term
    total = None
    for c in range(chunks):
        part = parts[c]
        log = sums[c * heads : (c + 1) * heads]
        end = log[:, CHUNK - 1 : CHUNK]
        total = end if total is None else total + end
        step = delta[:, part]
        grow_k[c] = stacked(jnp.exp(log)).T.astype(BF16)
        keep_k[c] = stacked(jnp.exp(end - log) * step).T.astype(BF16)
        off_k[c] = stacked((jnp.log(step) - log) * LOG2E).T.astype(BF16)
        log = log * LOG2E
        for i in range(width // LANES):
            log_rows[i, :, part] = log[i * per : (i + 1) * per]
    through_row = jnp.sum(jnp.where(same, jnp.exp(total), 0.0), axis=0, keepdims=True)
    t_all[0] = jnp.broadcast_to(
        jnp.concatenate([through_row, jnp.zeros((1, LANES - heads), F32)], axis=1), (8, LANES)
    )

    def tell(k):
        return pltpu.make_async_remote_copy(
            src_ref=t_all.at[0],
            dst_ref=t_all.at[k],
            send_sem=send_t.at[k - 1],
            recv_sem=recv_t.at[k - 1],
            device_id=(first_member + lax.rem(spot + k, TEAM), side),
            device_id_type=MESH,
        )

    for k in range(1, TEAM):
        tell(k).start()

    stack_row = iota((3 * heads, PIECE), 0)
    stack_head = lax.rem(stack_row, heads)

    @pl.loop(0, pieces)
    def _(p):
        sel_ref[p] = (stack_head == p * held + iota((3 * heads, PIECE), 1) // HEAD_DIM).astype(BF16)

    loads[2].wait()
    loads[3].wait()
    b_bf[...] = b_ref[...].astype(BF16)
    c_bf[...] = c_ref[...].astype(BF16)
    b_t_ref[...] = b_ref[...].T.astype(BF16)
    c_t_ref[...] = c_ref[...].T.astype(BF16)
    loads[4].wait()
    loads[5].wait()

    def core_swap(d, k):
        return pltpu.make_async_remote_copy(
            src_ref=own.at[d, k, mate_rows],
            dst_ref=own_in.at[d, k],
            send_sem=send_c.at[d, k],
            recv_sem=recv_c.at[d, k],
            device_id=(mate, side),
            device_id_type=MESH,
        )

    def along(d, k):
        return pltpu.make_async_remote_copy(
            src_ref=z_out.at[d, k],
            dst_ref=z_in.at[d, k],
            send_sem=send_z.at[d, k],
            recv_sem=recv_z.at[d, k],
            device_id=(me + TEAM if d == 0 else me - TEAM, side),
            device_id_type=MESH,
        )

    def crossing(d, k):
        return pltpu.make_async_remote_copy(
            src_ref=x_out.at[d, k],
            dst_ref=x_in.at[d, k],
            send_sem=send_x.at[d, k],
            recv_sem=recv_x.at[d, k],
            device_id=(across, side),
            device_id_type=MESH,
        )

    def hand_over(d, k):
        return pltpu.make_async_remote_copy(
            src_ref=core_out.at[d, k],
            dst_ref=entry.at[d, k, my_rows],
            send_sem=send_d.at[d, k],
            recv_sem=recv_d.at[d, k],
            device_id=(mate, side),
            device_id_type=MESH,
        )

    leads = [core == 0, core == 1]
    near = [column == 0, column == 1]
    place = [row, teams - 1 - row]

    def own_unit(p):
        lanes = piece_lanes(p)
        sel = sel_ref[p]
        through, fwd, bwd = [], [], []
        for c in range(chunks):
            part = parts[c]
            grow_x = nn(grow_k[c], sel)
            keep_x = nn(keep_k[c], sel)
            kept = (x_ref[part, lanes].astype(F32) * keep_x).astype(BF16)
            grown = (g_ref[part, lanes].astype(F32) * grow_x).astype(BF16)
            grow_x_ref[part, lanes] = grow_x
            keep_x_ref[part, lanes] = keep_x
            kept_ref[part, lanes] = kept
            grown_ref[part, lanes] = grown
            through.append(grow_x[CHUNK - 1 : CHUNK, :])
            fwd.append(nn(b_t_ref[:, part], kept))
            bwd.append(nn(c_t_ref[:, part], grown))
            chunk_own[0, c, p] = fwd[c]
            chunk_own[1, c, p] = bwd[c]
        total_f, total_b = fwd[0], bwd[chunks - 1]
        for c in range(1, chunks):
            total_f = through[c] * total_f + fwd[c]
        for c in reversed(range(chunks - 1)):
            total_b = through[c] * total_b + bwd[c]
        own[0, p] = total_f
        own[1, p] = total_b
        core_swap(0, p).start()
        core_swap(1, p).start()

    def gather(k, d):
        lanes = piece_lanes(k)
        core_swap(d, k).wait_recv()
        mine, theirs = own[d, k, my_rows], own_in[d, k]
        first = jnp.where(leads[d], mine, theirs)
        second = jnp.where(leads[d], theirs, mine)
        pair_sum[d, k] = factor[d, 1, 0:1, lanes] * first + second

    def pass_on(k, d):
        lanes = piece_lanes(k)

        @pl.when(place[d] == 0)
        def _():
            z_in[d, k] = jnp.zeros((half, PIECE), F32)

        @pl.when(place[d] > 0)
        def _():
            along(d, k).wait_recv()

        before, mine = z_in[d, k], pair_sum[d, k]

        @pl.when(place[d] < teams - 1)
        def _():
            z_out[d, k] = plane[0:1, lanes] * before + factor[d, 2, 0:1, lanes] * mine
            along(d, k).start()

        x_out[d, k] = jnp.where(near[d], factor[d, 3, 0:1, lanes] * before + mine, before).astype(BF16)
        crossing(d, k).start()

    def settle(k, d):
        lanes = piece_lanes(k)
        crossing(d, k).wait_recv()
        before, other = z_in[d, k], x_in[d, k].astype(F32)
        into = jnp.where(near[d], before + other, factor[d, 3, 0:1, lanes] * before + other)
        first = jnp.where(leads[d], own[d, k, my_rows], own_in[d, k])
        after = factor[d, 0, 0:1, lanes] * into + first
        entry[d, k, my_rows] = jnp.where(leads[d], into, after)
        core_out[d, k] = jnp.where(leads[d], after, into)
        hand_over(d, k).start()

    def stage(step, offset, act, d):
        k = step - offset

        @pl.when((k >= 0) & (k < pieces))
        def _():
            act(k, d)

    def exchange(step):
        for d in range(2):
            stage(step, 1, gather, d)
            stage(step, 1 + HOP_LAPS * place[d], pass_on, d)
            stage(step, 1 + HOP_LAPS * place[d] + LAST_LAPS, settle, d)

    own_unit(0)

    for k in range(1, TEAM):
        tell(k).wait_recv()
    loads[6].wait()
    skip_row = jnp.broadcast_to(skip_ref[...], (8, heads))

    def over_lanes(value):
        return jnp.concatenate([part.astype(F32) for part in split(value, 3)], axis=1).astype(BF16)

    spread_rows = [over_lanes(t_all[k][:, :heads]) for k in range(TEAM)] + [over_lanes(skip_row)]
    spread_rows = jnp.concatenate([value.astype(F32) for value in spread_rows], axis=0).astype(BF16)

    @pl.loop(0, pieces)
    def _(p):
        lanes = piece_lanes(p)
        lifted = nn(spread_rows, sel_ref[p])
        for k in range(TEAM):
            t_lanes[k, :, lanes] = lifted[8 * k : 8 * k + 8]
        skip_x[:, lanes] = lifted[8 * TEAM : 8 * TEAM + 8]

    def through_of(member):
        return t_lanes[lax.rem(spot - member + TEAM, TEAM)]

    t0, t1, t2, t3 = [through_of(member) for member in range(TEAM)]
    pair0, pair1 = t0 * t1, t2 * t3
    low, high = jnp.where(column == 0, t0, t2), jnp.where(column == 0, t1, t3)
    plane[...] = pair0 * pair1
    factor[0, 0], factor[0, 1] = low, high
    factor[1, 0], factor[1, 1] = high, low
    factor[0, 2] = jnp.where(near[0], pair1, 1.0)
    factor[1, 2] = jnp.where(near[1], pair0, 1.0)
    factor[0, 3], factor[1, 3] = pair0, pair1

    @pl.loop(1, pieces)
    def _(p):
        own_unit(p)
        exchange(p)

    causal = iota((CHUNK, CHUNK), 1) >= iota((CHUNK, CHUNK), 0)
    for part in parts:
        gram_t[part] = jnp.where(causal, fine(nt, b_ref[part], c_ref[part]), 0.0)
    dgram_t[...] = jnp.zeros_like(dgram_t)
    pairs = width // LANES
    low_lanes = (iota((1, LANES), 1) < HEAD_DIM).astype(BF16)
    high_lanes = (iota((1, LANES), 1) >= HEAD_DIM).astype(BF16)
    wide_head = lax.rem(iota((3 * heads, per * CHUNK), 0), heads)

    def within_unit(i):
        lanes = pl.ds(pl.multiple_of(i * LANES, LANES), LANES)
        picks = (wide_head == i * per + iota((3 * heads, per * CHUNK), 1) // CHUNK).astype(BF16)
        for c in range(chunks):
            part = parts[c]
            g_part = g_ref[part, lanes]
            both = jnp.concatenate([g_part * low_lanes, g_part * high_lanes], axis=0)
            pair = nt(x_ref[part, lanes], both)
            offset = nn(off_k[c], picks)
            gram = gram_t[part]
            weighed = []
            total = None
            for j in range(per):
                columns = slice(j * CHUNK, (j + 1) * CHUNK)
                weight = jnp.exp2(offset[:, columns] + log_rows[i, j : j + 1, part])
                bent = weight * gram
                value = weight * pair[:, columns]
                total = value if total is None else total + value
                row_u[i, j : j + 1, part] = jnp.sum(bent * pair[:, columns], axis=0, keepdims=True)
                weighed.append(bent.astype(BF16))
            dgram_t[part] += total
            inside[part, lanes] = nn(jnp.concatenate(weighed, axis=1), both)

    @pl.loop(0, pairs)
    def _(i):
        within_unit(i)
        exchange(pieces + i)

    for load in loads[7:]:
        load.wait()
    for e in range(experts):
        w_load(e, side).wait()
    capacity = act_ref.shape[1]
    before = (iota((length, length), 0) < iota((length, length), 1)).astype(BF16)

    def pick_slots(e):
        named = ids_ref[...] == side * experts + e
        hit = jnp.sum(named.astype(F32), axis=0, keepdims=True)
        rank = nn(jnp.broadcast_to(hit, (16, length)).astype(BF16), before)[0:1, :]
        place_row = jnp.where(hit > 0.5, rank, -1.0)
        picked = iota((capacity, length), 0).astype(F32) == place_row
        chosen_ref[e] = picked.astype(BF16)
        prob = jnp.sum(jnp.where(named, probs_ref[...], 0.0), axis=0, keepdims=True)
        weight = jnp.sum(jnp.where(picked, prob, 0.0), axis=1, keepdims=True)
        weight_ref[e] = jnp.broadcast_to(weight, (capacity, LANES))

    blocks = product.shape[0]
    block = product.shape[2]
    joined = block // hidden

    def w_rows(i):
        return pl.ds(pl.multiple_of(i * block, block), block)

    @pl.loop(0, blocks)
    def _(i):
        for j in range(joined):
            pick_slots(i * joined + j)
        product[i] = nt(g_ref[...], w_ref[w_rows(i)])
        exchange(pieces + pairs + i)

    def owner_of(k):
        return lax.rem(side + n_exp - k, n_exp)

    for e in range(experts):
        w_load(e, owner_of(1)).start()

    laps = pieces + pairs + blocks
    needed = pieces + HOP_LAPS * (teams - 1) + LAST_LAPS + 1

    if needed > laps:
        @pl.loop(laps, needed)
        def _(step):
            exchange(step)

    for part in parts:
        pull = jnp.where(causal, dgram_t[part], 0.0)
        part_b[part] = fine(nn, pull, c_ref[part])
        part_c[part] = fine(nn, pull.T, b_ref[part])
    end_ref[...] = jnp.zeros_like(end_ref)
    lane_head = lax.rem(iota((16, 4 * PIECE), 1), PIECE) // HEAD_DIM
    lane_kind = iota((16, 4 * PIECE), 1) // (2 * PIECE)
    gather_rows = (iota((16, 4 * PIECE), 0) == lane_head + held * lane_kind).astype(BF16)

    def across_unit(p):
        lanes = piece_lanes(p)
        hand_over(0, p).wait_recv()
        hand_over(1, p).wait_recv()
        through = [grow_x_ref[(c + 1) * CHUNK - 1 : (c + 1) * CHUNK, lanes] for c in range(chunks)]
        states = [entry[0, p]]
        for c in range(chunks):
            states.append(through[c] * states[c] + chunk_own[0, c, p])
        grads = [None] * chunks + [entry[1, p]]
        for c in reversed(range(1, chunks)):
            grads[c] = through[c] * grads[c + 1] + chunk_own[1, c, p]
        skip = skip_x[0:1, lanes]
        for c in range(chunks):
            part = parts[c]
            state, grad = states[c].astype(BF16), grads[c + 1].astype(BF16)
            x_part, g_part = x_ref[part, lanes].astype(F32), g_ref[part, lanes].astype(F32)
            from_grad = nn(b_bf[part], grad) * keep_x_ref[part, lanes]
            from_state = nn(c_bf[part], state) * grow_x_ref[part, lanes]
            part_c[part] += nt(grown_ref[part, lanes], state)
            part_b[part] += nt(kept_ref[part, lanes], grad)
            inner = inside[part, lanes] + from_grad
            grad_x_ref[part, lanes] = (inner + skip * g_part).astype(BF16)
            end_ref[c : c + 1, lanes] = jnp.sum(states[c + 1] * grads[c + 1], axis=0, keepdims=True)
            summed = split(x_part * inner, 2) + split(g_part * from_state, 2)
            uv_ref[p, :, part] = nt(gather_rows, jnp.concatenate(summed, axis=1))

    def grad_x_out(p):
        lanes = piece_lanes(p)
        return pltpu.make_async_copy(grad_x_ref.at[:, lanes], grad_x_any.at[:, lanes], save_x.at[p])

    @pl.loop(0, pieces)
    def _(p):
        across_unit(p)
        grad_x_out(p).start()

    share = grad_b_ref.shape[0]

    def shed(k, source, landing, send, recv):
        target = lax.rem(side + k, n_exp)
        return pltpu.make_async_remote_copy(
            src_ref=source.at[pl.ds(pl.multiple_of(target * share, share), share)],
            dst_ref=landing.at[k - 1],
            send_sem=send.at[k - 1],
            recv_sem=recv.at[k - 1],
            device_id=(me, target),
            device_id_type=MESH,
        )

    for k in range(1, n_exp):
        shed(k, part_b, land_b, send_p, recv_p).start()
        shed(k, part_c, land_c, send_q, recv_q).start()

    endings = None
    for piece in split(end_ref[...], 2):
        term = None
        for p in range(pieces):
            value = nt(piece[:, p * PIECE : (p + 1) * PIECE], sel_ref[p, 0:heads])
            term = value if term is None else term + value
        endings = term if endings is None else endings + term
    endings = endings.T
    v_rows = jnp.concatenate([uv_ref[p, 0:held] for p in range(pieces)], axis=0)
    u_rows = jnp.concatenate([uv_ref[p, held : 2 * held] for p in range(pieces)], axis=0)
    net = jnp.concatenate([row_u[i] for i in range(pairs)], axis=0) + u_rows - v_rows
    lower = (iota((CHUNK, CHUNK), 0) >= iota((CHUNK, CHUNK), 1)).astype(BF16)
    rows = jnp.concatenate([net[:, part] for part in parts], axis=0)
    sums = None
    for piece in split(rows, 3):
        term = nn(piece, lower)
        sums = term if sums is None else sums + term
    for c in range(chunks):
        part = parts[c]
        drift = sums[c * heads : (c + 1) * heads] + endings[:, c : c + 1]
        grad_delta_ref[:, part] = v_rows[:, part] / delta_ref[:, part] + rate * drift

    grad_delta_out = pltpu.make_async_copy(grad_delta_ref, grad_delta_any, save_sem.at[0])
    grad_delta_out.start()

    for k in range(1, n_exp):
        for e in range(experts):
            if k > 1:
                w_load(e, owner_of(k)).start()
            w_load(e, owner_of(k)).wait()
        for p in range(sends):
            to_partner(k, p).wait_recv()

            @pl.loop(0, blocks)
            def _(i):
                product[i] += nt(g_in[k - 1, p], w_ref[w_rows(i), p * sent : (p + 1) * sent])

    act_out = [
        pltpu.make_async_copy(grad_act_ref.at[e], grad_act_any.at[e], save_act.at[e])
        for e in range(experts)
    ]
    for e in range(experts):
        inner = None
        for piece in split(product[e // joined, :, (e % joined) * hidden : (e % joined + 1) * hidden], 2):
            term = nn(chosen_ref[e], piece)
            inner = term if inner is None else inner + term
        grad_act_ref[e] = (weight_ref[e][:, 0:1] * inner).astype(BF16)
        act_out[e].start()
        scored = act_ref[e].astype(F32) * inner
        ones = jnp.ones((16, scored.shape[1]), BF16)
        summed = None
        for piece in split(scored, 2):
            term = nt(ones, piece)
            summed = term if summed is None else summed + term
        grad_slots_ref[e : e + 1, :] = summed[0:1, :]

    mine = pl.ds(pl.multiple_of(side * share, share), share)
    total_b, total_c = part_b[mine], part_c[mine]
    for k in range(1, n_exp):
        shed(k, part_b, land_b, send_p, recv_p).wait_recv()
        shed(k, part_c, land_c, send_q, recv_q).wait_recv()
        total_b = total_b + land_b[k - 1]
        total_c = total_c + land_c[k - 1]
    grad_b_ref[...] = total_b
    grad_c_ref[...] = total_c

    last = [
        pltpu.make_async_copy(grad_b_ref, grad_b_any, save_sem.at[1]),
        pltpu.make_async_copy(grad_c_ref, grad_c_any, save_sem.at[2]),
        pltpu.make_async_copy(grad_slots_ref, grad_slots_any, save_sem.at[3]),
    ]
    for copy in last:
        copy.start()

    for k in range(1, n_exp):
        shed(k, part_b, land_b, send_p, recv_p).wait_send()
        shed(k, part_c, land_c, send_q, recv_q).wait_send()
        for p in range(sends):
            to_partner(k, p).wait_send()
    for k in range(1, TEAM):
        tell(k).wait_send()

    @pl.loop(0, pieces)
    def _(p):
        grad_x_out(p).wait()
        for d in range(2):
            core_swap(d, p).wait_send()
            crossing(d, p).wait_send()
            hand_over(d, p).wait_send()

            @pl.when(place[d] < teams - 1)
            def _():
                along(d, p).wait_send()

    for copy in act_out + [grad_delta_out] + last:
        copy.wait()


def store_kernel(count, *refs):
    sources, targets, held = refs[:count], refs[count : 2 * count], refs[2 * count : 3 * count]
    load_sem, save_sem = refs[3 * count :]
    pairs = []
    for source, target, buffer in zip(sources, targets, held):
        rows = source.shape[0]
        cut = rows // STORE_CUTS if rows % (8 * STORE_CUTS) == 0 and source.dtype == BF16 else rows
        for start in range(0, rows, cut):
            pairs.append([ref.at[start : start + cut] for ref in (source, buffer, target)])
    loads = [pltpu.make_async_copy(a, b, load_sem.at[i]) for i, (a, b, _) in enumerate(pairs)]
    saves = [pltpu.make_async_copy(b, c, save_sem.at[i]) for i, (_, b, c) in enumerate(pairs)]
    for load in loads:
        load.start()
    for load, save in zip(loads, saves):
        load.wait()
        save.start()
    for save in saves:
        save.wait()


def per_device(
    n_ctx, n_exp,
    feature_in, grad_out, delta, decay_log, skip_gain, b_proj, c_proj,
    route_ids, route_probs, w_down, saved_act,
):
    length, width = feature_in.shape
    heads = delta.shape[0]
    nstate = b_proj.shape[1]
    experts, hidden, full = w_down.shape
    capacity = saved_act.shape[2]
    topk = route_ids.shape[1]
    share = length // n_exp
    others = n_exp - 1
    chunks = length // CHUNK
    pieces = width // PIECE
    half = nstate // 2
    sent = min(SENT, width)
    sends = width // sent
    joined = 2 - experts % 2
    hbm = pl.BlockSpec(memory_space=pltpu.HBM)
    dma = pltpu.SemaphoreType.DMA
    inputs = (
        feature_in, grad_out, delta, decay_log[None, :], skip_gain[None, :], b_proj, c_proj,
        route_ids.T, route_probs.T, saved_act[0], w_down,
    )
    shard = jax.ShapeDtypeStruct((share, nstate), F32)
    shapes = (
        jax.ShapeDtypeStruct((length, width), BF16),
        jax.ShapeDtypeStruct((heads, length), F32),
        shard,
        shard,
        jax.ShapeDtypeStruct((experts, capacity, hidden), BF16),
        jax.ShapeDtypeStruct((experts, capacity), F32),
    )
    by_state = pltpu.VMEM((length, nstate), F32)
    per = LANES // HEAD_DIM
    by_pair = pltpu.VMEM((heads // per, per, length), F32)
    wide = pltpu.VMEM((length, width), F32)
    narrow = pltpu.VMEM((length, width), BF16)
    halves = pltpu.VMEM((2, pieces, half, PIECE), F32)
    halves_bf = pltpu.VMEM((2, pieces, half, PIECE), BF16)
    whole = pltpu.VMEM((2, pieces, nstate, PIECE), F32)
    results = pl.pallas_call(
        partial(block_kernel, n_ctx, n_exp),
        out_shape=shapes,
        in_specs=[hbm] * len(inputs),
        out_specs=(hbm,) * len(shapes),
        scratch_shapes=[pltpu.VMEM(value.shape, value.dtype) for value in shapes + inputs[:-1]]
        + [pltpu.VMEM((experts * hidden, width), BF16)]
        + [
            pltpu.VMEM((others, sends, length, sent), BF16),
            pltpu.VMEM((TEAM, 8, LANES), F32),
            pltpu.VMEM((TEAM, 8, width), F32),
            pltpu.VMEM((2, 4, 8, width), F32),
            pltpu.VMEM((8, width), F32),
            pltpu.VMEM((8, width), F32),
            pltpu.VMEM((pieces, 3 * heads, PIECE), BF16),
        ]
        + [pltpu.VMEM((chunks, CHUNK, 3 * heads), BF16)] * 3
        + [by_pair]
        + [pltpu.VMEM((length, nstate), BF16)] * 2
        + [pltpu.VMEM((nstate, length), BF16)] * 2
        + [pltpu.VMEM((length, CHUNK), F32)] * 2
        + [by_pair]
        + [pltpu.VMEM((pieces, 16, length), F32), pltpu.VMEM((8, width), F32)]
        + [by_state] * 2
        + [pltpu.VMEM((others, share, nstate), F32)] * 2
        + [pltpu.VMEM((2, chunks, pieces, nstate, PIECE), F32)]
        + [whole]
        + [halves] * 4
        + [halves_bf] * 2
        + [halves, whole]
        + [wide] * 2
        + [narrow] * 2
        + [wide]
        + [
            pltpu.VMEM((experts // joined, length, joined * hidden), F32),
            pltpu.VMEM((experts, capacity, length), BF16),
            pltpu.VMEM((experts, capacity, LANES), F32),
        ]
        + [dma((10,)), dma((experts,)), dma((pieces,)), dma((experts,)), dma((4,))]
        + [dma((others, sends))] * 2
        + [dma((TEAM - 1,))] * 2
        + [dma((2, pieces))] * 8
        + [dma((others,))] * 4,
        compiler_params=pltpu.CompilerParams(
            collective_id=0, has_side_effects=True, vmem_limit_bytes=60 << 20
        ),
        name="block_grads",
    )(*inputs)
    grad_x, grad_delta, grad_b, grad_c, grad_act, grad_slots = pl.pallas_call(
        partial(store_kernel, len(shapes)),
        out_shape=shapes,
        in_specs=[hbm] * len(shapes),
        out_specs=(hbm,) * len(shapes),
        scratch_shapes=[pltpu.VMEM(value.shape, value.dtype) for value in shapes]
        + [dma((len(shapes) + STORE_CUTS,))] * 2,
        compiler_params=pltpu.CompilerParams(vmem_limit_bytes=60 << 20),
        name="store",
    )(*results)
    return (grad_x, grad_delta, grad_b, grad_c, grad_act[None], grad_slots[None])


def solution(mesh):
    placed = (
        P("ctx", "exp"),
        P("ctx", "exp"),
        P("exp", "ctx"),
        P("exp"),
        P("exp"),
        P("ctx", None),
        P("ctx", None),
        P("ctx", None),
        P("ctx", None),
        P("exp", None, None),
        P("ctx", "exp", None, None),
    )
    return jax.shard_map(
        partial(per_device, mesh.shape["ctx"], mesh.shape["exp"]),
        mesh=mesh,
        in_specs=placed,
        out_specs=(
            P("ctx", "exp"),
            P("exp", "ctx"),
            P(("ctx", "exp"), None),
            P(("ctx", "exp"), None),
            P("ctx", "exp", None, None),
            P("ctx", "exp", None),
        ),
        check_vma=False,
    )
```

```python
from functools import partial

import jax
import jax.numpy as jnp
from jax import lax
from jax.experimental import pallas as pl
from jax.experimental.pallas import tpu as pltpu
from jax.sharding import PartitionSpec as P

HEAD_DIM = 64
CHUNK = 128
LANES = 128
PIECE = 256
SENT = 256
TEAM = 4
STORE_CUTS = 4
FIRST_LAP = 2
HOP_LAPS = 5
LAST_LAPS = 4
HAND_LAPS = 2
PAIRS = 2
LOG2E = 1.4426950408889634
F32 = jnp.float32
BF16 = jnp.bfloat16
MESH = pl.DeviceIdType.MESH


def nn(a, b):
    return lax.dot_general(a, b, (((1,), (0,)), ((), ())), preferred_element_type=F32)


def nt(a, b):
    return lax.dot_general(a, b, (((1,), (1,)), ((), ())), preferred_element_type=F32)


def split(value, count):
    parts = []
    for _ in range(count):
        part = value.astype(BF16)
        parts.append(part)
        value = value - part.astype(F32)
    return parts


def fine(dot, a, b):
    a_hi, a_lo = split(a, 2)
    b_hi, b_lo = split(b, 2)
    return dot(a_hi, b_hi) + (dot(a_hi, b_lo) + dot(a_lo, b_hi))


def stacked(value):
    return jnp.concatenate([part.astype(F32) for part in split(value, 3)], axis=0)


def iota(shape, dim):
    return lax.broadcasted_iota(jnp.int32, shape, dim)


def block_kernel(
    n_ctx, n_exp,
    x_any, g_any, delta_any, decay_any, skip_any, b_any, c_any, ids_any, probs_any, act_any, w_any,
    grad_x_any, grad_delta_any, grad_b_any, grad_c_any, grad_act_any, grad_slots_any,
    grad_x_ref, grad_delta_ref, grad_b_ref, grad_c_ref, grad_act_ref, grad_slots_ref,
    x_ref, g_ref, delta_ref, decay_ref, skip_ref, b_ref, c_ref, ids_ref, probs_ref, act_ref, w_ref,
    g_in, t_all, t_lanes, factor, plane, skip_x, sel_ref,
    lift_k, off_k, log_rows, b_bf, c_bf, b_t_ref, c_t_ref,
    gram_t, dgram_t, row_u, uv_ref, end_ref, part_b, part_c, out_b, out_c, land_b, land_c,
    chunk_own, own, own_in, pair_sum, z_in, z_out, x_out, x_in, core_out, entry,
    grow_x_ref, keep_x_ref, kept_ref, grown_ref, inside, product, act_sum, chosen_ref, weight_ref,
    load_sem, load_w, save_x, save_act, save_sem, send_g, recv_g, send_t, recv_t, send_c, recv_c, send_z, recv_z,
    send_x, recv_x, send_d, recv_d, send_p, recv_p, send_q, recv_q,
):
    me, side = lax.axis_index("ctx"), lax.axis_index("exp")
    teams = n_ctx // TEAM
    core, column, row = lax.rem(me, 2), lax.rem(me // 2, 2), me // TEAM
    spot = lax.rem(me, TEAM)
    first_member = me - spot
    mate = me + 1 - 2 * core
    across = me + 2 - 4 * column

    barrier = pltpu.get_barrier_semaphore()

    def greet(ctx, exp):
        pl.semaphore_signal(barrier, inc=1, device_id=(ctx, exp), device_id_type=MESH)

    for k in range(1, n_exp):
        greet(me, lax.rem(side + k, n_exp))
    for k in range(1, TEAM):
        greet(first_member + lax.rem(spot + k, TEAM), side)

    @pl.when(row > 0)
    def _():
        greet(me - TEAM, side)

    @pl.when(row < teams - 1)
    def _():
        greet(me + TEAM, side)

    arrays = [
        (delta_any, delta_ref), (decay_any, decay_ref), (b_any, b_ref), (c_any, c_ref),
        (x_any, x_ref), (g_any, g_ref), (skip_any, skip_ref), (ids_any, ids_ref),
        (probs_any, probs_ref), (act_any, act_ref),
    ]
    loads = [
        pltpu.make_async_copy(src, dst, load_sem.at[i]) for i, (src, dst) in enumerate(arrays)
    ]
    for load in loads:
        load.start()
    experts, hidden = w_any.shape[0], w_any.shape[1]
    width = x_ref.shape[1]

    def w_load(e, owner):
        columns = pl.ds(pl.multiple_of(owner * width, width), width)
        return pltpu.make_async_copy(
            w_any.at[e, :, columns], w_ref.at[pl.ds(e * hidden, hidden)], load_w.at[e]
        )

    for e in range(experts):
        w_load(e, side).start()

    met = n_exp - 1 + TEAM - 1 + (row > 0).astype(jnp.int32) + (row < teams - 1).astype(jnp.int32)
    pl.semaphore_wait(barrier, met)

    length = x_ref.shape[0]
    sent = g_in.shape[3]
    sends = width // sent

    def to_partner(k, p):
        return pltpu.make_async_remote_copy(
            src_ref=g_any.at[:, pl.ds(p * sent, sent)],
            dst_ref=g_in.at[k - 1, p],
            send_sem=send_g.at[k - 1, p],
            recv_sem=recv_g.at[k - 1, p],
            device_id=(me, lax.rem(side + k, n_exp)),
            device_id_type=MESH,
        )

    for p in range(sends):
        for k in range(1, n_exp):
            to_partner(k, p).start()

    heads = delta_ref.shape[0]
    chunks = length // CHUNK
    parts = [slice(c * CHUNK, (c + 1) * CHUNK) for c in range(chunks)]
    pieces = width // PIECE
    per = LANES // HEAD_DIM
    held = PIECE // HEAD_DIM
    nstate = b_ref.shape[1]
    half = nstate // 2
    my_rows = pl.ds(pl.multiple_of(core * half, half), half)
    mate_rows = pl.ds(pl.multiple_of((1 - core) * half, half), half)

    def piece_lanes(p):
        return pl.ds(pl.multiple_of(p * PIECE, PIECE), PIECE)

    loads[0].wait()
    loads[1].wait()
    delta = delta_ref[...]
    rate_row = -jnp.exp(decay_ref[...])
    same = iota((heads, heads), 0) == iota((heads, heads), 1)
    rate = jnp.sum(jnp.where(same, rate_row, 0.0), axis=1, keepdims=True)
    upper = (iota((CHUNK, CHUNK), 0) <= iota((CHUNK, CHUNK), 1)).astype(BF16)
    pace = delta * rate
    rows = jnp.concatenate([pace[:, part] for part in parts], axis=0)
    sums = None
    for piece in split(rows, 3):
        term = nn(piece, upper)
        sums = term if sums is None else sums + term
    total = None
    for c in range(chunks):
        part = parts[c]
        log = sums[c * heads : (c + 1) * heads]
        end = log[:, CHUNK - 1 : CHUNK]
        total = end if total is None else total + end
        step = delta[:, part]
        lift_k[part] = stacked(jnp.exp(log)).T.astype(BF16)
        lift_k[length + c * CHUNK : length + (c + 1) * CHUNK] = (
            stacked(jnp.exp(end - log) * step).T.astype(BF16)
        )
        off_k[part] = stacked((jnp.log(step) - log) * LOG2E).T.astype(BF16)
        log = log * LOG2E
        for i in range(width // LANES):
            log_rows[i, :, part] = log[i * per : (i + 1) * per]
    through_row = jnp.sum(jnp.where(same, jnp.exp(total), 0.0), axis=0, keepdims=True)
    t_all[0] = jnp.broadcast_to(
        jnp.concatenate([through_row, jnp.zeros((1, LANES - heads), F32)], axis=1), (8, LANES)
    )

    def tell(k):
        return pltpu.make_async_remote_copy(
            src_ref=t_all.at[0],
            dst_ref=t_all.at[k],
            send_sem=send_t.at[k - 1],
            recv_sem=recv_t.at[k - 1],
            device_id=(first_member + lax.rem(spot + k, TEAM), side),
            device_id_type=MESH,
        )

    for k in range(1, TEAM):
        tell(k).start()

    stack_row = iota((3 * heads, PIECE), 0)
    stack_head = lax.rem(stack_row, heads)

    @pl.loop(0, pieces)
    def _(p):
        sel_ref[p] = (stack_head == p * held + iota((3 * heads, PIECE), 1) // HEAD_DIM).astype(BF16)

    loads[2].wait()
    loads[3].wait()
    b_bf[...] = b_ref[...].astype(BF16)
    c_bf[...] = c_ref[...].astype(BF16)
    b_t_ref[...] = b_ref[...].T.astype(BF16)
    c_t_ref[...] = c_ref[...].T.astype(BF16)
    loads[4].wait()
    loads[5].wait()

    def core_swap(d, k):
        return pltpu.make_async_remote_copy(
            src_ref=own.at[d, k, mate_rows],
            dst_ref=own_in.at[d, k],
            send_sem=send_c.at[d, k],
            recv_sem=recv_c.at[d, k],
            device_id=(mate, side),
            device_id_type=MESH,
        )

    def along(d, k):
        return pltpu.make_async_remote_copy(
            src_ref=z_out.at[d, k],
            dst_ref=z_in.at[d, k],
            send_sem=send_z.at[d, k],
            recv_sem=recv_z.at[d, k],
            device_id=(me + TEAM if d == 0 else me - TEAM, side),
            device_id_type=MESH,
        )

    def crossing(d, k):
        return pltpu.make_async_remote_copy(
            src_ref=x_out.at[d, k],
            dst_ref=x_in.at[d, k],
            send_sem=send_x.at[d, k],
            recv_sem=recv_x.at[d, k],
            device_id=(across, side),
            device_id_type=MESH,
        )

    def hand_over(d, k):
        return pltpu.make_async_remote_copy(
            src_ref=core_out.at[d, k],
            dst_ref=entry.at[d, k, my_rows],
            send_sem=send_d.at[d, k],
            recv_sem=recv_d.at[d, k],
            device_id=(mate, side),
            device_id_type=MESH,
        )

    leads = [core == 0, core == 1]
    near = [column == 0, column == 1]
    place = [row, teams - 1 - row]

    def own_unit(p):
        lanes = piece_lanes(p)
        sel = sel_ref[p]
        through, fwd, bwd = [], [], []
        lifted = nn(lift_k[...], sel)
        grow_x_ref[:, lanes] = lifted[:length]
        keep_x_ref[:, lanes] = lifted[length:]
        for c in range(chunks):
            part = parts[c]
            grow_x = lifted[part]
            keep_x = lifted[length + c * CHUNK : length + (c + 1) * CHUNK]
            kept = (x_ref[part, lanes].astype(F32) * keep_x).astype(BF16)
            grown = (g_ref[part, lanes].astype(F32) * grow_x).astype(BF16)
            kept_ref[part, lanes] = kept
            grown_ref[part, lanes] = grown
            through.append(grow_x[CHUNK - 1 : CHUNK, :])
            fwd.append(nn(b_t_ref[:, part], kept))
            bwd.append(nn(c_t_ref[:, part], grown))
            chunk_own[0, c, p] = fwd[c]
            chunk_own[1, c, p] = bwd[c]
        total_f, total_b = fwd[0], bwd[chunks - 1]
        for c in range(1, chunks):
            total_f = through[c] * total_f + fwd[c]
        for c in reversed(range(chunks - 1)):
            total_b = through[c] * total_b + bwd[c]
        own[0, p] = total_f
        own[1, p] = total_b
        core_swap(0, p).start()
        core_swap(1, p).start()

    def gather(k, d):
        lanes = piece_lanes(k)
        core_swap(d, k).wait_recv()
        mine, theirs = own[d, k, my_rows], own_in[d, k]
        first = jnp.where(leads[d], mine, theirs)
        second = jnp.where(leads[d], theirs, mine)
        pair_sum[d, k] = factor[d, 1, 0:1, lanes] * first + second

    def pass_on(k, d):
        lanes = piece_lanes(k)

        @pl.when(place[d] == 0)
        def _():
            z_in[d, k] = jnp.zeros((half, PIECE), F32)

        @pl.when(place[d] > 0)
        def _():
            along(d, k).wait_recv()

        before, mine = z_in[d, k], pair_sum[d, k]

        @pl.when(place[d] < teams - 1)
        def _():
            z_out[d, k] = plane[0:1, lanes] * before + factor[d, 2, 0:1, lanes] * mine
            along(d, k).start()

        x_out[d, k] = jnp.where(near[d], factor[d, 3, 0:1, lanes] * before + mine, before).astype(BF16)
        crossing(d, k).start()

    def settle(k, d):
        lanes = piece_lanes(k)
        crossing(d, k).wait_recv()
        before, other = z_in[d, k], x_in[d, k].astype(F32)
        into = jnp.where(near[d], before + other, factor[d, 3, 0:1, lanes] * before + other)
        first = jnp.where(leads[d], own[d, k, my_rows], own_in[d, k])
        after = factor[d, 0, 0:1, lanes] * into + first
        entry[d, k, my_rows] = jnp.where(leads[d], into, after)
        core_out[d, k] = jnp.where(leads[d], after, into)
        hand_over(d, k).start()

    def stage(step, offset, act, d):
        k = step - offset

        @pl.when((k >= 0) & (k < pieces))
        def _():
            act(k, d)

    def exchange(step):
        for d in range(2):
            stage(step, FIRST_LAP, gather, d)
            stage(step, FIRST_LAP + HOP_LAPS * place[d], pass_on, d)
            stage(step, FIRST_LAP + HOP_LAPS * place[d] + LAST_LAPS, settle, d)

    early = min(FIRST_LAP, pieces)
    for p in range(early):
        own_unit(p)

    for k in range(1, TEAM):
        tell(k).wait_recv()
    loads[6].wait()
    skip_row = jnp.broadcast_to(skip_ref[...], (8, heads))

    def over_lanes(value):
        return jnp.concatenate([part.astype(F32) for part in split(value, 3)], axis=1).astype(BF16)

    spread_rows = [over_lanes(t_all[k][:, :heads]) for k in range(TEAM)] + [over_lanes(skip_row)]
    spread_rows = jnp.concatenate([value.astype(F32) for value in spread_rows], axis=0).astype(BF16)

    @pl.loop(0, pieces)
    def _(p):
        lanes = piece_lanes(p)
        lifted = nn(spread_rows, sel_ref[p])
        for k in range(TEAM):
            t_lanes[k, :, lanes] = lifted[8 * k : 8 * k + 8]
        skip_x[:, lanes] = lifted[8 * TEAM : 8 * TEAM + 8]

    def through_of(member):
        return t_lanes[lax.rem(spot - member + TEAM, TEAM)]

    t0, t1, t2, t3 = [through_of(member) for member in range(TEAM)]
    pair0, pair1 = t0 * t1, t2 * t3
    low, high = jnp.where(column == 0, t0, t2), jnp.where(column == 0, t1, t3)
    plane[...] = pair0 * pair1
    factor[0, 0], factor[0, 1] = low, high
    factor[1, 0], factor[1, 1] = high, low
    factor[0, 2] = jnp.where(near[0], pair1, 1.0)
    factor[1, 2] = jnp.where(near[1], pair0, 1.0)
    factor[0, 3], factor[1, 3] = pair0, pair1

    @pl.loop(early, pieces)
    def _(p):
        own_unit(p)
        exchange(p)

    for load in loads[7:]:
        load.wait()
    for e in range(experts):
        w_load(e, side).wait()
    capacity = act_ref.shape[1]
    before = (iota((length, length), 0) < iota((length, length), 1)).astype(BF16)

    def pick_slots(e):
        named = ids_ref[...] == side * experts + e
        hit = jnp.sum(named.astype(F32), axis=0, keepdims=True)
        rank = nn(jnp.broadcast_to(hit, (16, length)).astype(BF16), before)[0:1, :]
        place_row = jnp.where(hit > 0.5, rank, -1.0)
        picked = iota((capacity, length), 0).astype(F32) == place_row
        chosen_ref[e] = picked.astype(BF16)
        prob = jnp.sum(jnp.where(named, probs_ref[...], 0.0), axis=0, keepdims=True)
        weight = jnp.sum(jnp.where(picked, prob, 0.0), axis=1, keepdims=True)
        weight_ref[e] = jnp.broadcast_to(weight, (capacity, LANES))

    blocks = product.shape[0]
    block = product.shape[2]
    joined = block // hidden

    def w_rows(i):
        return pl.ds(pl.multiple_of(i * block, block), block)

    @pl.loop(0, blocks)
    def _(i):
        for j in range(joined):
            pick_slots(i * joined + j)
        product[i] = nt(g_ref[...], w_ref[w_rows(i)])
        exchange(pieces + 2 * i)
        exchange(pieces + 2 * i + 1)

    def owner_of(k):
        return lax.rem(side + n_exp - k, n_exp)

    for e in range(experts):
        w_load(e, owner_of(1)).start()

    causal = iota((CHUNK, CHUNK), 1) >= iota((CHUNK, CHUNK), 0)
    for part in parts:
        gram_t[part] = jnp.where(causal, fine(nt, b_ref[part], c_ref[part]), 0.0)
    dgram_t[...] = jnp.zeros_like(dgram_t)
    pairs = width // LANES
    low_lanes = (iota((1, LANES), 1) < HEAD_DIM).astype(BF16)
    high_lanes = (iota((1, LANES), 1) >= HEAD_DIM).astype(BF16)
    wide_head = lax.rem(iota((3 * heads, per * CHUNK), 0), heads)

    def within_unit(i):
        lanes = pl.ds(pl.multiple_of(i * LANES, LANES), LANES)
        picks = (wide_head == i * per + iota((3 * heads, per * CHUNK), 1) // CHUNK).astype(BF16)
        offsets = nn(off_k[...], picks)
        for c in range(chunks):
            part = parts[c]
            g_part = g_ref[part, lanes]
            both = jnp.concatenate([g_part * low_lanes, g_part * high_lanes], axis=0)
            pair = nt(x_ref[part, lanes], both)
            offset = offsets[part]
            gram = gram_t[part]
            weighed = []
            total = None
            for j in range(per):
                columns = slice(j * CHUNK, (j + 1) * CHUNK)
                weight = jnp.exp2(offset[:, columns] + log_rows[i, j : j + 1, part])
                bent = weight * gram
                value = weight * pair[:, columns]
                total = value if total is None else total + value
                row_u[i, j : j + 1, part] = jnp.sum(bent * pair[:, columns], axis=0, keepdims=True)
                weighed.append(bent.astype(BF16))
            dgram_t[part] += total
            inside[part, lanes] = nn(jnp.concatenate(weighed, axis=1), both)

    turns = pairs // PAIRS

    @pl.loop(0, turns)
    def _(i):
        for j in range(PAIRS):
            within_unit(i * PAIRS + j)
        exchange(pieces + 2 * blocks + i)

    order = [(k, p) for k in range(1, n_exp) for p in range(sends)]
    groups = []
    for k in range(1, n_exp):
        mine = [p for p in range(sends) if (k, p) != order[-1]]
        groups += [(k, mine[i : i + 2]) for i in range(0, len(mine), 2)]

    def other_columns(k, group, act):
        if group[0] == 0:
            for e in range(experts):
                if k > 1:
                    w_load(e, owner_of(k)).start()
                w_load(e, owner_of(k)).wait()
        for p in group:
            to_partner(k, p).wait_recv()

        @pl.loop(0, blocks)
        def _(i):
            columns = slice(group[0] * sent, (group[-1] + 1) * sent)
            grads = jnp.concatenate([g_in[k - 1, p] for p in group], axis=1)
            product[i] += nt(grads, w_ref[w_rows(i), columns])
            act(i)

    base = pieces + 2 * blocks + turns
    ahead = groups[: len(groups) // 2]
    for n, (k, group) in enumerate(ahead):
        other_columns(k, group, lambda i, n=n: exchange(base + n * blocks + i))

    laps = base + len(ahead) * blocks
    needed = max(laps, FIRST_LAP + HOP_LAPS * (teams - 1) + LAST_LAPS + HAND_LAPS)

    if needed > laps:
        @pl.loop(laps, needed)
        def _(step):
            exchange(step)

    for part in parts:
        pull = jnp.where(causal, dgram_t[part], 0.0)
        part_b[part] = fine(nn, pull, c_ref[part])
        part_c[part] = fine(nn, pull.T, b_ref[part])
    end_ref[...] = jnp.zeros_like(end_ref)
    lane_head = lax.rem(iota((16, 4 * PIECE), 1), PIECE) // HEAD_DIM
    lane_kind = iota((16, 4 * PIECE), 1) // (2 * PIECE)
    gather_rows = (iota((16, 4 * PIECE), 0) == lane_head + held * lane_kind).astype(BF16)

    def across_unit(p):
        lanes = piece_lanes(p)
        hand_over(0, p).wait_recv()
        hand_over(1, p).wait_recv()
        through = [grow_x_ref[(c + 1) * CHUNK - 1 : (c + 1) * CHUNK, lanes] for c in range(chunks)]
        states = [entry[0, p]]
        for c in range(chunks):
            states.append(through[c] * states[c] + chunk_own[0, c, p])
        grads = [None] * chunks + [entry[1, p]]
        for c in reversed(range(1, chunks)):
            grads[c] = through[c] * grads[c + 1] + chunk_own[1, c, p]
        skip = skip_x[0:1, lanes]
        for c in range(chunks):
            part = parts[c]
            state, grad = states[c].astype(BF16), grads[c + 1].astype(BF16)
            x_part, g_part = x_ref[part, lanes].astype(F32), g_ref[part, lanes].astype(F32)
            from_grad = nn(b_bf[part], grad) * keep_x_ref[part, lanes]
            from_state = nn(c_bf[part], state) * grow_x_ref[part, lanes]
            part_c[part] += nt(grown_ref[part, lanes], state)
            part_b[part] += nt(kept_ref[part, lanes], grad)
            inner = inside[part, lanes] + from_grad
            grad_x_ref[part, lanes] = (inner + skip * g_part).astype(BF16)
            end_ref[c : c + 1, lanes] = jnp.sum(states[c + 1] * grads[c + 1], axis=0, keepdims=True)
            summed = split(x_part * inner, 2) + split(g_part * from_state, 2)
            uv_ref[p, :, part] = nt(gather_rows, jnp.concatenate(summed, axis=1))

    def grad_x_out(p):
        lanes = piece_lanes(p)
        return pltpu.make_async_copy(grad_x_ref.at[:, lanes], grad_x_any.at[:, lanes], save_x.at[p])

    @pl.loop(0, pieces)
    def _(p):
        exchange(needed + p)
        across_unit(p)
        grad_x_out(p).start()

    share = grad_b_ref.shape[0]

    def shed(k, source, landing, send, recv):
        target = lax.rem(side + k, n_exp)
        return pltpu.make_async_remote_copy(
            src_ref=source.at[pl.ds(pl.multiple_of(target * share, share), share)],
            dst_ref=landing.at[k - 1],
            send_sem=send.at[k - 1],
            recv_sem=recv.at[k - 1],
            device_id=(me, target),
            device_id_type=MESH,
        )

    out_b[...] = part_b[...].astype(BF16)
    out_c[...] = part_c[...].astype(BF16)
    for k in range(1, n_exp):
        shed(k, out_b, land_b, send_p, recv_p).start()
        shed(k, out_c, land_c, send_q, recv_q).start()

    endings = None
    for piece in split(end_ref[...], 2):
        term = None
        for p in range(pieces):
            value = nt(piece[:, p * PIECE : (p + 1) * PIECE], sel_ref[p, 0:heads])
            term = value if term is None else term + value
        endings = term if endings is None else endings + term
    endings = endings.T
    v_rows = jnp.concatenate([uv_ref[p, 0:held] for p in range(pieces)], axis=0)
    u_rows = jnp.concatenate([uv_ref[p, held : 2 * held] for p in range(pieces)], axis=0)
    net = jnp.concatenate([row_u[i] for i in range(pairs)], axis=0) + u_rows - v_rows
    lower = (iota((CHUNK, CHUNK), 0) >= iota((CHUNK, CHUNK), 1)).astype(BF16)
    rows = jnp.concatenate([net[:, part] for part in parts], axis=0)
    sums = None
    for piece in split(rows, 3):
        term = nn(piece, lower)
        sums = term if sums is None else sums + term
    for c in range(chunks):
        part = parts[c]
        drift = sums[c * heads : (c + 1) * heads] + endings[:, c : c + 1]
        grad_delta_ref[:, part] = v_rows[:, part] / delta_ref[:, part] + rate * drift

    grad_delta_out = pltpu.make_async_copy(grad_delta_ref, grad_delta_any, save_sem.at[0])
    grad_delta_out.start()

    for k, group in groups[len(ahead) :]:
        other_columns(k, group, lambda i: None)
    for e in range(experts):
        total = None
        hidden_columns = slice((e % joined) * hidden, (e % joined + 1) * hidden)
        for piece in split(product[e // joined, :, hidden_columns], 2):
            term = nn(chosen_ref[e], piece)
            total = term if total is None else total + term
        act_sum[e] = total
    k, p = order[-1]
    to_partner(k, p).wait_recv()
    act_out = [
        pltpu.make_async_copy(grad_act_ref.at[e], grad_act_any.at[e], save_act.at[e])
        for e in range(experts)
    ]
    for e in range(experts):
        taken = nn(chosen_ref[e], g_in[k - 1, p]).astype(BF16)
        inner = act_sum[e] + nt(taken, w_ref[e * hidden : (e + 1) * hidden, p * sent : (p + 1) * sent])
        grad_act_ref[e] = (weight_ref[e][:, 0:1] * inner).astype(BF16)
        act_out[e].start()
        scored = act_ref[e].astype(F32) * inner
        ones = jnp.ones((16, scored.shape[1]), BF16)
        summed = None
        for piece in split(scored, 2):
            term = nt(ones, piece)
            summed = term if summed is None else summed + term
        grad_slots_ref[e : e + 1, :] = summed[0:1, :]

    mine = pl.ds(pl.multiple_of(side * share, share), share)
    total_b, total_c = part_b[mine], part_c[mine]
    for k in range(1, n_exp):
        shed(k, out_b, land_b, send_p, recv_p).wait_recv()
        shed(k, out_c, land_c, send_q, recv_q).wait_recv()
        total_b = total_b + land_b[k - 1].astype(F32)
        total_c = total_c + land_c[k - 1].astype(F32)
    grad_b_ref[...] = total_b
    grad_c_ref[...] = total_c

    last = [
        pltpu.make_async_copy(grad_b_ref, grad_b_any, save_sem.at[1]),
        pltpu.make_async_copy(grad_c_ref, grad_c_any, save_sem.at[2]),
        pltpu.make_async_copy(grad_slots_ref, grad_slots_any, save_sem.at[3]),
    ]
    for copy in last:
        copy.start()

    for k in range(1, n_exp):
        shed(k, out_b, land_b, send_p, recv_p).wait_send()
        shed(k, out_c, land_c, send_q, recv_q).wait_send()
        for p in range(sends):
            to_partner(k, p).wait_send()
    for k in range(1, TEAM):
        tell(k).wait_send()

    @pl.loop(0, pieces)
    def _(p):
        grad_x_out(p).wait()
        for d in range(2):
            core_swap(d, p).wait_send()
            crossing(d, p).wait_send()
            hand_over(d, p).wait_send()

            @pl.when(place[d] < teams - 1)
            def _():
                along(d, p).wait_send()

    for copy in act_out + [grad_delta_out] + last:
        copy.wait()


def store_kernel(count, *refs):
    sources, targets, held = refs[:count], refs[count : 2 * count], refs[2 * count : 3 * count]
    load_sem, save_sem = refs[3 * count :]
    pairs = []
    for source, target, buffer in zip(sources, targets, held):
        rows = source.shape[0]
        cut = rows // STORE_CUTS if rows % (8 * STORE_CUTS) == 0 and source.dtype == BF16 else rows
        for start in range(0, rows, cut):
            pairs.append([ref.at[start : start + cut] for ref in (source, buffer, target)])
    loads = [pltpu.make_async_copy(a, b, load_sem.at[i]) for i, (a, b, _) in enumerate(pairs)]
    saves = [pltpu.make_async_copy(b, c, save_sem.at[i]) for i, (_, b, c) in enumerate(pairs)]
    for load in loads:
        load.start()
    for load, save in zip(loads, saves):
        load.wait()
        save.start()
    for save in saves:
        save.wait()


def per_device(
    n_ctx, n_exp,
    feature_in, grad_out, delta, decay_log, skip_gain, b_proj, c_proj,
    route_ids, route_probs, w_down, saved_act,
):
    length, width = feature_in.shape
    heads = delta.shape[0]
    nstate = b_proj.shape[1]
    experts, hidden, full = w_down.shape
    capacity = saved_act.shape[2]
    topk = route_ids.shape[1]
    share = length // n_exp
    others = n_exp - 1
    chunks = length // CHUNK
    pieces = width // PIECE
    half = nstate // 2
    sent = min(SENT, width)
    sends = width // sent
    joined = 2 - experts % 2
    hbm = pl.BlockSpec(memory_space=pltpu.HBM)
    dma = pltpu.SemaphoreType.DMA
    inputs = (
        feature_in, grad_out, delta, decay_log[None, :], skip_gain[None, :], b_proj, c_proj,
        route_ids.T, route_probs.T, saved_act[0], w_down,
    )
    shard = jax.ShapeDtypeStruct((share, nstate), F32)
    shapes = (
        jax.ShapeDtypeStruct((length, width), BF16),
        jax.ShapeDtypeStruct((heads, length), F32),
        shard,
        shard,
        jax.ShapeDtypeStruct((experts, capacity, hidden), BF16),
        jax.ShapeDtypeStruct((experts, capacity), F32),
    )
    by_state = pltpu.VMEM((length, nstate), F32)
    per = LANES // HEAD_DIM
    by_pair = pltpu.VMEM((heads // per, per, length), F32)
    wide = pltpu.VMEM((length, width), F32)
    narrow = pltpu.VMEM((length, width), BF16)
    halves = pltpu.VMEM((2, pieces, half, PIECE), F32)
    halves_bf = pltpu.VMEM((2, pieces, half, PIECE), BF16)
    whole = pltpu.VMEM((2, pieces, nstate, PIECE), F32)
    results = pl.pallas_call(
        partial(block_kernel, n_ctx, n_exp),
        out_shape=shapes,
        in_specs=[hbm] * len(inputs),
        out_specs=(hbm,) * len(shapes),
        scratch_shapes=[pltpu.VMEM(value.shape, value.dtype) for value in shapes + inputs[:-1]]
        + [pltpu.VMEM((experts * hidden, width), BF16)]
        + [
            pltpu.VMEM((others, sends, length, sent), BF16),
            pltpu.VMEM((TEAM, 8, LANES), F32),
            pltpu.VMEM((TEAM, 8, width), F32),
            pltpu.VMEM((2, 4, 8, width), F32),
            pltpu.VMEM((8, width), F32),
            pltpu.VMEM((8, width), F32),
            pltpu.VMEM((pieces, 3 * heads, PIECE), BF16),
        ]
        + [pltpu.VMEM((2 * length, 3 * heads), BF16), pltpu.VMEM((length, 3 * heads), BF16)]
        + [by_pair]
        + [pltpu.VMEM((length, nstate), BF16)] * 2
        + [pltpu.VMEM((nstate, length), BF16)] * 2
        + [pltpu.VMEM((length, CHUNK), F32)] * 2
        + [by_pair]
        + [pltpu.VMEM((pieces, 16, length), F32), pltpu.VMEM((8, width), F32)]
        + [by_state] * 2
        + [pltpu.VMEM((length, nstate), BF16)] * 2
        + [pltpu.VMEM((others, share, nstate), BF16)] * 2
        + [pltpu.VMEM((2, chunks, pieces, nstate, PIECE), F32)]
        + [whole]
        + [halves] * 4
        + [halves_bf] * 2
        + [halves, whole]
        + [wide] * 2
        + [narrow] * 2
        + [wide]
        + [
            pltpu.VMEM((experts // joined, length, joined * hidden), F32),
            pltpu.VMEM((experts, capacity, hidden), F32),
            pltpu.VMEM((experts, capacity, length), BF16),
            pltpu.VMEM((experts, capacity, LANES), F32),
        ]
        + [dma((10,)), dma((experts,)), dma((pieces,)), dma((experts,)), dma((4,))]
        + [dma((others, sends))] * 2
        + [dma((TEAM - 1,))] * 2
        + [dma((2, pieces))] * 8
        + [dma((others,))] * 4,
        compiler_params=pltpu.CompilerParams(
            collective_id=0, has_side_effects=True, vmem_limit_bytes=60 << 20
        ),
        name="block_grads",
    )(*inputs)
    grad_x, grad_delta, grad_b, grad_c, grad_act, grad_slots = pl.pallas_call(
        partial(store_kernel, len(shapes)),
        out_shape=shapes,
        in_specs=[hbm] * len(shapes),
        out_specs=(hbm,) * len(shapes),
        scratch_shapes=[pltpu.VMEM(value.shape, value.dtype) for value in shapes]
        + [dma((len(shapes) + STORE_CUTS,))] * 2,
        compiler_params=pltpu.CompilerParams(vmem_limit_bytes=60 << 20),
        name="store",
    )(*results)
    return (grad_x, grad_delta, grad_b, grad_c, grad_act[None], grad_slots[None])


def solution(mesh):
    placed = (
        P("ctx", "exp"),
        P("ctx", "exp"),
        P("exp", "ctx"),
        P("exp"),
        P("exp"),
        P("ctx", None),
        P("ctx", None),
        P("ctx", None),
        P("ctx", None),
        P("exp", None, None),
        P("ctx", "exp", None, None),
    )
    return jax.shard_map(
        partial(per_device, mesh.shape["ctx"], mesh.shape["exp"]),
        mesh=mesh,
        in_specs=placed,
        out_specs=(
            P("ctx", "exp"),
            P("exp", "ctx"),
            P(("ctx", "exp"), None),
            P(("ctx", "exp"), None),
            P("ctx", "exp", None, None),
            P("ctx", "exp", None),
        ),
        check_vma=False,
    )
```

```python
from functools import partial

import jax
import jax.numpy as jnp
from jax import lax
from jax.experimental import pallas as pl
from jax.experimental.pallas import tpu as pltpu
from jax.sharding import PartitionSpec as P

HEAD_DIM = 64
CHUNK = 128
LANES = 128
PIECE = 256
SENT = 256
TEAM = 4
STORE_CUTS = 4
FIRST_LAP = 2
HOP_LAPS = 4
LAST_LAPS = 4
HAND_LAPS = 2
PAIRS = 2
LOG2E = 1.4426950408889634
F32 = jnp.float32
BF16 = jnp.bfloat16
MESH = pl.DeviceIdType.MESH


def nn(a, b):
    return lax.dot_general(a, b, (((1,), (0,)), ((), ())), preferred_element_type=F32)


def nt(a, b):
    return lax.dot_general(a, b, (((1,), (1,)), ((), ())), preferred_element_type=F32)


def split(value, count):
    parts = []
    for _ in range(count):
        part = value.astype(BF16)
        parts.append(part)
        value = value - part.astype(F32)
    return parts


def fine(dot, a, b):
    a_hi, a_lo = split(a, 2)
    b_hi, b_lo = split(b, 2)
    return dot(a_hi, b_hi) + (dot(a_hi, b_lo) + dot(a_lo, b_hi))


def stacked(value):
    return jnp.concatenate([part.astype(F32) for part in split(value, 3)], axis=0)


def iota(shape, dim):
    return lax.broadcasted_iota(jnp.int32, shape, dim)


def block_kernel(
    n_ctx, n_exp,
    x_any, g_any, delta_any, decay_any, skip_any, b_any, c_any, ids_any, probs_any, act_any, w_any,
    grad_x_any, grad_delta_any, grad_b_any, grad_c_any, grad_act_any, grad_slots_any,
    grad_x_ref, grad_delta_ref, grad_b_ref, grad_c_ref, grad_act_ref, grad_slots_ref,
    x_ref, g_ref, delta_ref, decay_ref, skip_ref, b_ref, c_ref, ids_ref, probs_ref, act_ref, w_ref,
    g_in, t_all, t_lanes, factor, plane, skip_x, sel_ref,
    lift_k, off_k, log_rows, b_two, c_two, b_t_ref, c_t_ref,
    gram_t, dgram_t, row_u, uv_ref, end_ref, part_b, part_c, out_b, out_c, land_b, land_c,
    chunk_own, own, own_in, pair_sum, z_in, z_out, x_out, x_in, core_out, entry,
    grow_x_ref, keep_x_ref, kept_ref, grown_ref, inside, product, act_sum, chosen_ref, weight_ref,
    load_sem, load_w, save_x, save_act, save_sem, send_g, recv_g, send_t, recv_t, send_c, recv_c, send_z, recv_z,
    send_x, recv_x, send_d, recv_d, send_p, recv_p, send_q, recv_q,
):
    me, side = lax.axis_index("ctx"), lax.axis_index("exp")
    teams = n_ctx // TEAM
    core, column, row = lax.rem(me, 2), lax.rem(me // 2, 2), me // TEAM
    spot = lax.rem(me, TEAM)
    first_member = me - spot
    mate = me + 1 - 2 * core
    across = me + 2 - 4 * column

    barrier = pltpu.get_barrier_semaphore()

    def greet(ctx, exp):
        pl.semaphore_signal(barrier, inc=1, device_id=(ctx, exp), device_id_type=MESH)

    for k in range(1, n_exp):
        greet(me, lax.rem(side + k, n_exp))
    for k in range(1, TEAM):
        greet(first_member + lax.rem(spot + k, TEAM), side)

    @pl.when(row > 0)
    def _():
        greet(me - TEAM, side)

    @pl.when(row < teams - 1)
    def _():
        greet(me + TEAM, side)

    arrays = [
        (delta_any, delta_ref), (decay_any, decay_ref), (b_any, b_ref), (c_any, c_ref),
        (x_any, x_ref), (g_any, g_ref), (skip_any, skip_ref), (ids_any, ids_ref),
        (probs_any, probs_ref), (act_any, act_ref),
    ]
    loads = [
        pltpu.make_async_copy(src, dst, load_sem.at[i]) for i, (src, dst) in enumerate(arrays)
    ]
    for load in loads:
        load.start()
    experts, hidden = w_any.shape[0], w_any.shape[1]
    width = x_ref.shape[1]

    def w_load(e, owner):
        columns = pl.ds(pl.multiple_of(owner * width, width), width)
        return pltpu.make_async_copy(
            w_any.at[e, :, columns], w_ref.at[pl.ds(e * hidden, hidden)], load_w.at[e]
        )

    for e in range(experts):
        w_load(e, side).start()

    met = n_exp - 1 + TEAM - 1 + (row > 0).astype(jnp.int32) + (row < teams - 1).astype(jnp.int32)
    pl.semaphore_wait(barrier, met)

    length = x_ref.shape[0]
    sent = g_in.shape[3]
    sends = width // sent

    def to_partner(k, p):
        return pltpu.make_async_remote_copy(
            src_ref=g_any.at[:, pl.ds(p * sent, sent)],
            dst_ref=g_in.at[k - 1, p],
            send_sem=send_g.at[k - 1, p],
            recv_sem=recv_g.at[k - 1, p],
            device_id=(me, lax.rem(side + k, n_exp)),
            device_id_type=MESH,
        )

    for p in range(sends):
        for k in range(1, n_exp):
            to_partner(k, p).start()

    heads = delta_ref.shape[0]
    chunks = length // CHUNK
    parts = [slice(c * CHUNK, (c + 1) * CHUNK) for c in range(chunks)]
    pieces = width // PIECE
    per = LANES // HEAD_DIM
    held = PIECE // HEAD_DIM
    nstate = b_ref.shape[1]
    half = nstate // 2
    my_rows = pl.ds(pl.multiple_of(core * half, half), half)
    mate_rows = pl.ds(pl.multiple_of((1 - core) * half, half), half)

    def piece_lanes(p):
        return pl.ds(pl.multiple_of(p * PIECE, PIECE), PIECE)

    loads[0].wait()
    loads[1].wait()
    delta = delta_ref[...]
    rate_row = -jnp.exp(decay_ref[...])
    same = iota((heads, heads), 0) == iota((heads, heads), 1)
    rate = jnp.sum(jnp.where(same, rate_row, 0.0), axis=1, keepdims=True)
    upper = (iota((CHUNK, CHUNK), 0) <= iota((CHUNK, CHUNK), 1)).astype(BF16)
    pace = delta * rate
    rows = jnp.concatenate([pace[:, part] for part in parts], axis=0)
    sums = None
    for piece in split(rows, 3):
        term = nn(piece, upper)
        sums = term if sums is None else sums + term
    total = None
    for c in range(chunks):
        part = parts[c]
        log = sums[c * heads : (c + 1) * heads]
        end = log[:, CHUNK - 1 : CHUNK]
        total = end if total is None else total + end
        step = delta[:, part]
        lift_k[part] = stacked(jnp.exp(log)).T.astype(BF16)
        lift_k[length + c * CHUNK : length + (c + 1) * CHUNK] = (
            stacked(jnp.exp(end - log) * step).T.astype(BF16)
        )
        off_k[part] = stacked((jnp.log(step) - log) * LOG2E).T.astype(BF16)
        log = log * LOG2E
        for i in range(width // LANES):
            log_rows[i, :, part] = log[i * per : (i + 1) * per]
    through_row = jnp.sum(jnp.where(same, jnp.exp(total), 0.0), axis=0, keepdims=True)
    t_all[0] = jnp.broadcast_to(
        jnp.concatenate([through_row, jnp.zeros((1, LANES - heads), F32)], axis=1), (8, LANES)
    )

    def tell(k):
        return pltpu.make_async_remote_copy(
            src_ref=t_all.at[0],
            dst_ref=t_all.at[k],
            send_sem=send_t.at[k - 1],
            recv_sem=recv_t.at[k - 1],
            device_id=(first_member + lax.rem(spot + k, TEAM), side),
            device_id_type=MESH,
        )

    for k in range(1, TEAM):
        tell(k).start()

    stack_row = iota((3 * heads, PIECE), 0)
    stack_head = lax.rem(stack_row, heads)

    @pl.loop(0, pieces)
    def _(p):
        sel_ref[p] = (stack_head == p * held + iota((3 * heads, PIECE), 1) // HEAD_DIM).astype(BF16)

    loads[2].wait()
    loads[3].wait()
    b_two[...] = jnp.concatenate(split(b_ref[...], 2), axis=1)
    c_two[...] = jnp.concatenate(split(c_ref[...], 2), axis=1)
    b_t_ref[...] = b_ref[...].T.astype(BF16)
    c_t_ref[...] = c_ref[...].T.astype(BF16)
    loads[4].wait()
    loads[5].wait()

    def core_swap(d, k):
        return pltpu.make_async_remote_copy(
            src_ref=own.at[d, k, mate_rows],
            dst_ref=own_in.at[d, k],
            send_sem=send_c.at[d, k],
            recv_sem=recv_c.at[d, k],
            device_id=(mate, side),
            device_id_type=MESH,
        )

    def along(d, k):
        return pltpu.make_async_remote_copy(
            src_ref=z_out.at[d, k],
            dst_ref=z_in.at[d, k],
            send_sem=send_z.at[d, k],
            recv_sem=recv_z.at[d, k],
            device_id=(me + TEAM if d == 0 else me - TEAM, side),
            device_id_type=MESH,
        )

    def crossing(d, k):
        return pltpu.make_async_remote_copy(
            src_ref=x_out.at[d, k],
            dst_ref=x_in.at[d, k],
            send_sem=send_x.at[d, k],
            recv_sem=recv_x.at[d, k],
            device_id=(across, side),
            device_id_type=MESH,
        )

    def hand_over(d, k):
        return pltpu.make_async_remote_copy(
            src_ref=core_out.at[d, k],
            dst_ref=entry.at[d, k, my_rows],
            send_sem=send_d.at[d, k],
            recv_sem=recv_d.at[d, k],
            device_id=(mate, side),
            device_id_type=MESH,
        )

    leads = [core == 0, core == 1]
    near = [column == 0, column == 1]
    place = [row, teams - 1 - row]

    def own_unit(p):
        lanes = piece_lanes(p)
        sel = sel_ref[p]
        through, fwd, bwd = [], [], []
        lifted = nn(lift_k[...], sel)
        grow_x_ref[:, lanes] = lifted[:length]
        keep_x_ref[:, lanes] = lifted[length:]
        for c in range(chunks):
            part = parts[c]
            grow_x = lifted[part]
            keep_x = lifted[length + c * CHUNK : length + (c + 1) * CHUNK]
            kept = (x_ref[part, lanes].astype(F32) * keep_x).astype(BF16)
            grown = (g_ref[part, lanes].astype(F32) * grow_x).astype(BF16)
            kept_ref[part, lanes] = kept
            grown_ref[part, lanes] = grown
            through.append(grow_x[CHUNK - 1 : CHUNK, :])
            fwd.append(nn(b_t_ref[:, part], kept))
            bwd.append(nn(c_t_ref[:, part], grown))
            chunk_own[0, c, p] = fwd[c]
            chunk_own[1, c, p] = bwd[c]
        total_f, total_b = fwd[0], bwd[chunks - 1]
        for c in range(1, chunks):
            total_f = through[c] * total_f + fwd[c]
        for c in reversed(range(chunks - 1)):
            total_b = through[c] * total_b + bwd[c]
        own[0, p] = total_f
        own[1, p] = total_b
        core_swap(0, p).start()
        core_swap(1, p).start()

    def gather(k, d):
        lanes = piece_lanes(k)
        core_swap(d, k).wait_recv()
        mine, theirs = own[d, k, my_rows], own_in[d, k]
        first = jnp.where(leads[d], mine, theirs)
        second = jnp.where(leads[d], theirs, mine)
        pair_sum[d, k] = factor[d, 1, 0:1, lanes] * first + second

    def pass_on(k, d):
        lanes = piece_lanes(k)

        @pl.when(place[d] == 0)
        def _():
            z_in[d, k] = jnp.zeros((half, PIECE), BF16)

        @pl.when(place[d] > 0)
        def _():
            along(d, k).wait_recv()

        before, mine = z_in[d, k].astype(F32), pair_sum[d, k]

        @pl.when(place[d] < teams - 1)
        def _():
            sent_on = plane[0:1, lanes] * before + factor[d, 2, 0:1, lanes] * mine
            z_out[d, k] = sent_on.astype(BF16)
            along(d, k).start()

        x_out[d, k] = jnp.where(near[d], factor[d, 3, 0:1, lanes] * before + mine, before).astype(BF16)
        crossing(d, k).start()

    def settle(k, d):
        lanes = piece_lanes(k)
        crossing(d, k).wait_recv()
        before, other = z_in[d, k].astype(F32), x_in[d, k].astype(F32)
        into = jnp.where(near[d], before + other, factor[d, 3, 0:1, lanes] * before + other)
        first = jnp.where(leads[d], own[d, k, my_rows], own_in[d, k])
        after = factor[d, 0, 0:1, lanes] * into + first
        entry[d, k, my_rows] = jnp.where(leads[d], into, after)
        core_out[d, k] = jnp.where(leads[d], after, into)
        hand_over(d, k).start()

    def stage(step, offset, act, d):
        k = step - offset

        @pl.when((k >= 0) & (k < pieces))
        def _():
            act(k, d)

    def exchange(step):
        for d in range(2):
            stage(step, FIRST_LAP, gather, d)
            stage(step, FIRST_LAP + HOP_LAPS * place[d], pass_on, d)
            stage(step, FIRST_LAP + HOP_LAPS * place[d] + LAST_LAPS, settle, d)

    early = min(FIRST_LAP, pieces)
    for p in range(early):
        own_unit(p)

    for k in range(1, TEAM):
        tell(k).wait_recv()
    loads[6].wait()
    skip_row = jnp.broadcast_to(skip_ref[...], (8, heads))

    def over_lanes(value):
        return jnp.concatenate([part.astype(F32) for part in split(value, 3)], axis=1).astype(BF16)

    spread_rows = [over_lanes(t_all[k][:, :heads]) for k in range(TEAM)] + [over_lanes(skip_row)]
    spread_rows = jnp.concatenate([value.astype(F32) for value in spread_rows], axis=0).astype(BF16)

    @pl.loop(0, pieces)
    def _(p):
        lanes = piece_lanes(p)
        lifted = nn(spread_rows, sel_ref[p])
        for k in range(TEAM):
            t_lanes[k, :, lanes] = lifted[8 * k : 8 * k + 8]
        skip_x[:, lanes] = lifted[8 * TEAM : 8 * TEAM + 8]

    def through_of(member):
        return t_lanes[lax.rem(spot - member + TEAM, TEAM)]

    t0, t1, t2, t3 = [through_of(member) for member in range(TEAM)]
    pair0, pair1 = t0 * t1, t2 * t3
    low, high = jnp.where(column == 0, t0, t2), jnp.where(column == 0, t1, t3)
    plane[...] = pair0 * pair1
    factor[0, 0], factor[0, 1] = low, high
    factor[1, 0], factor[1, 1] = high, low
    factor[0, 2] = jnp.where(near[0], pair1, 1.0)
    factor[1, 2] = jnp.where(near[1], pair0, 1.0)
    factor[0, 3], factor[1, 3] = pair0, pair1

    @pl.loop(early, pieces)
    def _(p):
        own_unit(p)
        exchange(p)

    for load in loads[7:]:
        load.wait()
    for e in range(experts):
        w_load(e, side).wait()
    capacity = act_ref.shape[1]
    before = (iota((length, length), 0) < iota((length, length), 1)).astype(BF16)

    def pick_slots(e):
        named = ids_ref[...] == side * experts + e
        hit = jnp.sum(named.astype(F32), axis=0, keepdims=True)
        rank = nn(jnp.broadcast_to(hit, (16, length)).astype(BF16), before)[0:1, :]
        place_row = jnp.where(hit > 0.5, rank, -1.0)
        picked = iota((capacity, length), 0).astype(F32) == place_row
        chosen_ref[e] = picked.astype(BF16)
        prob = jnp.sum(jnp.where(named, probs_ref[...], 0.0), axis=0, keepdims=True)
        weight = jnp.sum(jnp.where(picked, prob, 0.0), axis=1, keepdims=True)
        weight_ref[e] = jnp.broadcast_to(weight, (capacity, LANES))

    blocks = product.shape[0]
    block = product.shape[2]
    joined = block // hidden

    def w_rows(i):
        return pl.ds(pl.multiple_of(i * block, block), block)

    @pl.loop(0, blocks)
    def _(i):
        for j in range(joined):
            pick_slots(i * joined + j)
        product[i] = nt(g_ref[...], w_ref[w_rows(i)])
        exchange(pieces + 2 * i)
        exchange(pieces + 2 * i + 1)

    def owner_of(k):
        return lax.rem(side + n_exp - k, n_exp)

    for e in range(experts):
        w_load(e, owner_of(1)).start()

    causal = iota((CHUNK, CHUNK), 1) >= iota((CHUNK, CHUNK), 0)
    for part in parts:
        gram_t[part] = jnp.where(causal, fine(nt, b_ref[part], c_ref[part]), 0.0)
    dgram_t[...] = jnp.zeros_like(dgram_t)
    pairs = width // LANES
    low_lanes = (iota((1, LANES), 1) < HEAD_DIM).astype(BF16)
    high_lanes = (iota((1, LANES), 1) >= HEAD_DIM).astype(BF16)
    wide_head = lax.rem(iota((3 * heads, per * CHUNK), 0), heads)

    def within_unit(i):
        lanes = pl.ds(pl.multiple_of(i * LANES, LANES), LANES)
        picks = (wide_head == i * per + iota((3 * heads, per * CHUNK), 1) // CHUNK).astype(BF16)
        offsets = nn(off_k[...], picks)
        for c in range(chunks):
            part = parts[c]
            g_part = g_ref[part, lanes]
            both = jnp.concatenate([g_part * low_lanes, g_part * high_lanes], axis=0)
            pair = nt(x_ref[part, lanes], both)
            offset = offsets[part]
            gram = gram_t[part]
            weighed = []
            total = None
            for j in range(per):
                columns = slice(j * CHUNK, (j + 1) * CHUNK)
                weight = jnp.exp2(offset[:, columns] + log_rows[i, j : j + 1, part])
                bent = weight * gram
                value = weight * pair[:, columns]
                total = value if total is None else total + value
                row_u[i, j : j + 1, part] = jnp.sum(bent * pair[:, columns], axis=0, keepdims=True)
                weighed.append(bent.astype(BF16))
            dgram_t[part] += total
            inside[part, lanes] = nn(jnp.concatenate(weighed, axis=1), both)

    turns = pairs // PAIRS

    @pl.loop(0, turns)
    def _(i):
        for j in range(PAIRS):
            within_unit(i * PAIRS + j)
        exchange(pieces + 2 * blocks + i)

    order = [(k, p) for k in range(1, n_exp) for p in range(sends)]
    groups = []
    for k in range(1, n_exp):
        mine = [p for p in range(sends) if (k, p) != order[-1]]
        groups += [(k, mine[i : i + 2]) for i in range(0, len(mine), 2)]

    def other_columns(k, group, act):
        if group[0] == 0:
            for e in range(experts):
                if k > 1:
                    w_load(e, owner_of(k)).start()
                w_load(e, owner_of(k)).wait()
        for p in group:
            to_partner(k, p).wait_recv()

        @pl.loop(0, blocks)
        def _(i):
            columns = slice(group[0] * sent, (group[-1] + 1) * sent)
            grads = jnp.concatenate([g_in[k - 1, p] for p in group], axis=1)
            product[i] += nt(grads, w_ref[w_rows(i), columns])
            act(i)

    base = pieces + 2 * blocks + turns
    ahead = groups[: len(groups) // 4]
    for n, (k, group) in enumerate(ahead):
        other_columns(k, group, lambda i, n=n: exchange(base + n * blocks + i))

    laps = base + len(ahead) * blocks
    needed = max(laps, FIRST_LAP + HOP_LAPS * (teams - 1) + LAST_LAPS + HAND_LAPS)

    if needed > laps:
        @pl.loop(laps, needed)
        def _(step):
            exchange(step)

    for part in parts:
        pull = jnp.where(causal, dgram_t[part], 0.0)
        part_b[part] = fine(nn, pull, c_ref[part])
        part_c[part] = fine(nn, pull.T, b_ref[part])
    end_ref[...] = jnp.zeros_like(end_ref)
    lane_head = lax.rem(iota((16, 4 * PIECE), 1), PIECE) // HEAD_DIM
    lane_kind = iota((16, 4 * PIECE), 1) // (2 * PIECE)
    gather_rows = (iota((16, 4 * PIECE), 0) == lane_head + held * lane_kind).astype(BF16)

    def across_unit(p):
        lanes = piece_lanes(p)
        hand_over(0, p).wait_recv()
        hand_over(1, p).wait_recv()
        through = [grow_x_ref[(c + 1) * CHUNK - 1 : (c + 1) * CHUNK, lanes] for c in range(chunks)]
        states = [entry[0, p]]
        for c in range(chunks):
            states.append(through[c] * states[c] + chunk_own[0, c, p])
        grads = [None] * chunks + [entry[1, p]]
        for c in reversed(range(1, chunks)):
            grads[c] = through[c] * grads[c + 1] + chunk_own[1, c, p]
        skip = skip_x[0:1, lanes]
        for c in range(chunks):
            part = parts[c]
            state, grad = states[c].astype(BF16), grads[c + 1].astype(BF16)
            x_part, g_part = x_ref[part, lanes].astype(F32), g_ref[part, lanes].astype(F32)
            keep_x, grow_x = keep_x_ref[part, lanes], grow_x_ref[part, lanes]
            from_grad = nn(b_two[part], jnp.concatenate([grad, grad], axis=0)) * keep_x
            from_state = nn(c_two[part], jnp.concatenate([state, state], axis=0)) * grow_x
            kept, grown = kept_ref[part, lanes], grown_ref[part, lanes]
            kept_two = jnp.concatenate([kept, (x_part * keep_x - kept.astype(F32)).astype(BF16)], axis=1)
            grown_two = jnp.concatenate([grown, (g_part * grow_x - grown.astype(F32)).astype(BF16)], axis=1)
            part_c[part] += nt(grown_two, jnp.concatenate([state, state], axis=1))
            part_b[part] += nt(kept_two, jnp.concatenate([grad, grad], axis=1))
            inner = inside[part, lanes] + from_grad
            grad_x_ref[part, lanes] = (inner + skip * g_part).astype(BF16)
            end_ref[c : c + 1, lanes] = jnp.sum(states[c + 1] * grads[c + 1], axis=0, keepdims=True)
            summed = split(x_part * inner, 2) + split(g_part * from_state, 2)
            uv_ref[p, :, part] = nt(gather_rows, jnp.concatenate(summed, axis=1))

    def grad_x_out(p):
        lanes = piece_lanes(p)
        return pltpu.make_async_copy(grad_x_ref.at[:, lanes], grad_x_any.at[:, lanes], save_x.at[p])

    @pl.loop(0, pieces)
    def _(p):
        exchange(needed + p)
        across_unit(p)
        grad_x_out(p).start()

    share = grad_b_ref.shape[0]

    def shed(k, source, landing, send, recv):
        target = lax.rem(side + k, n_exp)
        return pltpu.make_async_remote_copy(
            src_ref=source.at[pl.ds(pl.multiple_of(target * share, share), share)],
            dst_ref=landing.at[k - 1],
            send_sem=send.at[k - 1],
            recv_sem=recv.at[k - 1],
            device_id=(me, target),
            device_id_type=MESH,
        )

    out_b[...] = part_b[...].astype(BF16)
    out_c[...] = part_c[...].astype(BF16)
    for k in range(1, n_exp):
        shed(k, out_b, land_b, send_p, recv_p).start()
        shed(k, out_c, land_c, send_q, recv_q).start()

    endings = None
    for piece in split(end_ref[...], 2):
        term = None
        for p in range(pieces):
            value = nt(piece[:, p * PIECE : (p + 1) * PIECE], sel_ref[p, 0:heads])
            term = value if term is None else term + value
        endings = term if endings is None else endings + term
    endings = endings.T
    v_rows = jnp.concatenate([uv_ref[p, 0:held] for p in range(pieces)], axis=0)
    u_rows = jnp.concatenate([uv_ref[p, held : 2 * held] for p in range(pieces)], axis=0)
    net = jnp.concatenate([row_u[i] for i in range(pairs)], axis=0) + u_rows - v_rows
    lower = (iota((CHUNK, CHUNK), 0) >= iota((CHUNK, CHUNK), 1)).astype(BF16)
    rows = jnp.concatenate([net[:, part] for part in parts], axis=0)
    sums = None
    for piece in split(rows, 3):
        term = nn(piece, lower)
        sums = term if sums is None else sums + term
    for c in range(chunks):
        part = parts[c]
        drift = sums[c * heads : (c + 1) * heads] + endings[:, c : c + 1]
        grad_delta_ref[:, part] = v_rows[:, part] / delta_ref[:, part] + rate * drift

    grad_delta_out = pltpu.make_async_copy(grad_delta_ref, grad_delta_any, save_sem.at[0])
    grad_delta_out.start()

    for k, group in groups[len(ahead) :]:
        other_columns(k, group, lambda i: None)
    for e in range(experts):
        total = None
        hidden_columns = slice((e % joined) * hidden, (e % joined + 1) * hidden)
        for piece in split(product[e // joined, :, hidden_columns], 2):
            term = nn(chosen_ref[e], piece)
            total = term if total is None else total + term
        act_sum[e] = total
    k, p = order[-1]
    to_partner(k, p).wait_recv()
    act_out = [
        pltpu.make_async_copy(grad_act_ref.at[e], grad_act_any.at[e], save_act.at[e])
        for e in range(experts)
    ]
    for e in range(experts):
        taken = nn(chosen_ref[e], g_in[k - 1, p]).astype(BF16)
        inner = act_sum[e] + nt(taken, w_ref[e * hidden : (e + 1) * hidden, p * sent : (p + 1) * sent])
        grad_act_ref[e] = (weight_ref[e][:, 0:1] * inner).astype(BF16)
        act_out[e].start()
        scored = act_ref[e].astype(F32) * inner
        ones = jnp.ones((16, scored.shape[1]), BF16)
        summed = None
        for piece in split(scored, 2):
            term = nt(ones, piece)
            summed = term if summed is None else summed + term
        grad_slots_ref[e : e + 1, :] = summed[0:1, :]

    mine = pl.ds(pl.multiple_of(side * share, share), share)
    total_b, total_c = part_b[mine], part_c[mine]
    for k in range(1, n_exp):
        shed(k, out_b, land_b, send_p, recv_p).wait_recv()
        shed(k, out_c, land_c, send_q, recv_q).wait_recv()
        total_b = total_b + land_b[k - 1].astype(F32)
        total_c = total_c + land_c[k - 1].astype(F32)
    grad_b_ref[...] = total_b
    grad_c_ref[...] = total_c

    last = [
        pltpu.make_async_copy(grad_b_ref, grad_b_any, save_sem.at[1]),
        pltpu.make_async_copy(grad_c_ref, grad_c_any, save_sem.at[2]),
        pltpu.make_async_copy(grad_slots_ref, grad_slots_any, save_sem.at[3]),
    ]
    for copy in last:
        copy.start()

    for k in range(1, n_exp):
        shed(k, out_b, land_b, send_p, recv_p).wait_send()
        shed(k, out_c, land_c, send_q, recv_q).wait_send()
        for p in range(sends):
            to_partner(k, p).wait_send()
    for k in range(1, TEAM):
        tell(k).wait_send()

    @pl.loop(0, pieces)
    def _(p):
        grad_x_out(p).wait()
        for d in range(2):
            core_swap(d, p).wait_send()
            crossing(d, p).wait_send()
            hand_over(d, p).wait_send()

            @pl.when(place[d] < teams - 1)
            def _():
                along(d, p).wait_send()

    for copy in act_out + [grad_delta_out] + last:
        copy.wait()


def store_kernel(count, *refs):
    sources, targets, held = refs[:count], refs[count : 2 * count], refs[2 * count : 3 * count]
    load_sem, save_sem = refs[3 * count :]
    pairs = []
    for source, target, buffer in zip(sources, targets, held):
        rows = source.shape[0]
        cut = rows // STORE_CUTS if rows % (8 * STORE_CUTS) == 0 and source.dtype == BF16 else rows
        for start in range(0, rows, cut):
            pairs.append([ref.at[start : start + cut] for ref in (source, buffer, target)])
    loads = [pltpu.make_async_copy(a, b, load_sem.at[i]) for i, (a, b, _) in enumerate(pairs)]
    saves = [pltpu.make_async_copy(b, c, save_sem.at[i]) for i, (_, b, c) in enumerate(pairs)]
    for load in loads:
        load.start()
    for load, save in zip(loads, saves):
        load.wait()
        save.start()
    for save in saves:
        save.wait()


def per_device(
    n_ctx, n_exp,
    feature_in, grad_out, delta, decay_log, skip_gain, b_proj, c_proj,
    route_ids, route_probs, w_down, saved_act,
):
    length, width = feature_in.shape
    heads = delta.shape[0]
    nstate = b_proj.shape[1]
    experts, hidden, full = w_down.shape
    capacity = saved_act.shape[2]
    topk = route_ids.shape[1]
    share = length // n_exp
    others = n_exp - 1
    chunks = length // CHUNK
    pieces = width // PIECE
    half = nstate // 2
    sent = min(SENT, width)
    sends = width // sent
    joined = 2 - experts % 2
    hbm = pl.BlockSpec(memory_space=pltpu.HBM)
    dma = pltpu.SemaphoreType.DMA
    inputs = (
        feature_in, grad_out, delta, decay_log[None, :], skip_gain[None, :], b_proj, c_proj,
        route_ids.T, route_probs.T, saved_act[0], w_down,
    )
    shard = jax.ShapeDtypeStruct((share, nstate), F32)
    shapes = (
        jax.ShapeDtypeStruct((length, width), BF16),
        jax.ShapeDtypeStruct((heads, length), F32),
        shard,
        shard,
        jax.ShapeDtypeStruct((experts, capacity, hidden), BF16),
        jax.ShapeDtypeStruct((experts, capacity), F32),
    )
    by_state = pltpu.VMEM((length, nstate), F32)
    per = LANES // HEAD_DIM
    by_pair = pltpu.VMEM((heads // per, per, length), F32)
    wide = pltpu.VMEM((length, width), F32)
    narrow = pltpu.VMEM((length, width), BF16)
    halves = pltpu.VMEM((2, pieces, half, PIECE), F32)
    halves_bf = pltpu.VMEM((2, pieces, half, PIECE), BF16)
    whole = pltpu.VMEM((2, pieces, nstate, PIECE), F32)
    results = pl.pallas_call(
        partial(block_kernel, n_ctx, n_exp),
        out_shape=shapes,
        in_specs=[hbm] * len(inputs),
        out_specs=(hbm,) * len(shapes),
        scratch_shapes=[pltpu.VMEM(value.shape, value.dtype) for value in shapes + inputs[:-1]]
        + [pltpu.VMEM((experts * hidden, width), BF16)]
        + [
            pltpu.VMEM((others, sends, length, sent), BF16),
            pltpu.VMEM((TEAM, 8, LANES), F32),
            pltpu.VMEM((TEAM, 8, width), F32),
            pltpu.VMEM((2, 4, 8, width), F32),
            pltpu.VMEM((8, width), F32),
            pltpu.VMEM((8, width), F32),
            pltpu.VMEM((pieces, 3 * heads, PIECE), BF16),
        ]
        + [pltpu.VMEM((2 * length, 3 * heads), BF16), pltpu.VMEM((length, 3 * heads), BF16)]
        + [by_pair]
        + [pltpu.VMEM((length, 2 * nstate), BF16)] * 2
        + [pltpu.VMEM((nstate, length), BF16)] * 2
        + [pltpu.VMEM((length, CHUNK), F32)] * 2
        + [by_pair]
        + [pltpu.VMEM((pieces, 16, length), F32), pltpu.VMEM((8, width), F32)]
        + [by_state] * 2
        + [pltpu.VMEM((length, nstate), BF16)] * 2
        + [pltpu.VMEM((others, share, nstate), BF16)] * 2
        + [pltpu.VMEM((2, chunks, pieces, nstate, PIECE), F32)]
        + [whole]
        + [halves] * 2
        + [halves_bf] * 4
        + [halves, whole]
        + [wide] * 2
        + [narrow] * 2
        + [wide]
        + [
            pltpu.VMEM((experts // joined, length, joined * hidden), F32),
            pltpu.VMEM((experts, capacity, hidden), F32),
            pltpu.VMEM((experts, capacity, length), BF16),
            pltpu.VMEM((experts, capacity, LANES), F32),
        ]
        + [dma((10,)), dma((experts,)), dma((pieces,)), dma((experts,)), dma((4,))]
        + [dma((others, sends))] * 2
        + [dma((TEAM - 1,))] * 2
        + [dma((2, pieces))] * 8
        + [dma((others,))] * 4,
        compiler_params=pltpu.CompilerParams(
            collective_id=0, has_side_effects=True, vmem_limit_bytes=60 << 20
        ),
        name="block_grads",
    )(*inputs)
    grad_x, grad_delta, grad_b, grad_c, grad_act, grad_slots = pl.pallas_call(
        partial(store_kernel, len(shapes)),
        out_shape=shapes,
        in_specs=[hbm] * len(shapes),
        out_specs=(hbm,) * len(shapes),
        scratch_shapes=[pltpu.VMEM(value.shape, value.dtype) for value in shapes]
        + [dma((len(shapes) + STORE_CUTS,))] * 2,
        compiler_params=pltpu.CompilerParams(vmem_limit_bytes=60 << 20),
        name="store",
    )(*results)
    return (grad_x, grad_delta, grad_b, grad_c, grad_act[None], grad_slots[None])


def solution(mesh):
    placed = (
        P("ctx", "exp"),
        P("ctx", "exp"),
        P("exp", "ctx"),
        P("exp"),
        P("exp"),
        P("ctx", None),
        P("ctx", None),
        P("ctx", None),
        P("ctx", None),
        P("exp", None, None),
        P("ctx", "exp", None, None),
    )
    return jax.shard_map(
        partial(per_device, mesh.shape["ctx"], mesh.shape["exp"]),
        mesh=mesh,
        in_specs=placed,
        out_specs=(
            P("ctx", "exp"),
            P("exp", "ctx"),
            P(("ctx", "exp"), None),
            P(("ctx", "exp"), None),
            P("ctx", "exp", None, None),
            P("ctx", "exp", None),
        ),
        check_vma=False,
    )
```

```python
from functools import partial

import jax
import jax.numpy as jnp
from jax import lax
from jax.experimental import pallas as pl
from jax.experimental.pallas import tpu as pltpu
from jax.sharding import PartitionSpec as P

HEAD_DIM = 64
CHUNK = 128
LANES = 128
PIECE = 256
SENT = 256
TEAM = 4
STORE_CUTS = 4
FIRST_LAP = 2
HOP_LAPS = 4
LAST_LAPS = 4
HAND_LAPS = 2
PAIRS = 2
LOG2E = 1.4426950408889634
F32 = jnp.float32
BF16 = jnp.bfloat16
MESH = pl.DeviceIdType.MESH


def nn(a, b):
    return lax.dot_general(a, b, (((1,), (0,)), ((), ())), preferred_element_type=F32)


def nt(a, b):
    return lax.dot_general(a, b, (((1,), (1,)), ((), ())), preferred_element_type=F32)


def split(value, count):
    parts = []
    for _ in range(count):
        part = value.astype(BF16)
        parts.append(part)
        value = value - part.astype(F32)
    return parts


def fine(dot, a, b):
    a_hi, a_lo = split(a, 2)
    b_hi, b_lo = split(b, 2)
    return dot(a_hi, b_hi) + (dot(a_hi, b_lo) + dot(a_lo, b_hi))


def stacked(value):
    return jnp.concatenate([part.astype(F32) for part in split(value, 3)], axis=0)


def iota(shape, dim):
    return lax.broadcasted_iota(jnp.int32, shape, dim)


def block_kernel(
    n_ctx, n_exp,
    x_any, g_any, delta_any, decay_any, skip_any, b_any, c_any, ids_any, probs_any, act_any, w_any,
    grad_x_any, grad_delta_any, grad_b_any, grad_c_any, grad_act_any, grad_slots_any,
    grad_x_ref, grad_delta_ref, grad_b_ref, grad_c_ref, grad_act_ref, grad_slots_ref,
    x_ref, g_ref, delta_ref, decay_ref, skip_ref, b_ref, c_ref, ids_ref, probs_ref, act_ref, w_ref,
    g_in, t_all, t_lanes, factor, plane, skip_x, sel_ref,
    lift_k, off_k, log_rows, b_two, c_two, b_t_ref, c_t_ref,
    gram_t, dgram_t, row_u, uv_ref, end_ref, part_b, part_c, out_b, out_c, land_b, land_c,
    chunk_own, own, own_in, pair_sum, z_in, z_out, x_out, x_in, core_out, entry,
    grow_x_ref, keep_x_ref, kept_ref, grown_ref, inside, product, act_sum, chosen_ref, weight_ref,
    load_sem, load_w, save_x, save_act, save_sem, send_g, recv_g, send_t, recv_t, send_c, recv_c, send_z, recv_z,
    send_x, recv_x, send_d, recv_d, send_p, recv_p, send_q, recv_q,
):
    me, side = lax.axis_index("ctx"), lax.axis_index("exp")
    teams = n_ctx // TEAM
    core, column, row = lax.rem(me, 2), lax.rem(me // 2, 2), me // TEAM
    spot = lax.rem(me, TEAM)
    first_member = me - spot
    mate = me + 1 - 2 * core
    across = me + 2 - 4 * column

    barrier = pltpu.get_barrier_semaphore()

    def greet(ctx, exp):
        pl.semaphore_signal(barrier, inc=1, device_id=(ctx, exp), device_id_type=MESH)

    for k in range(1, n_exp):
        greet(me, lax.rem(side + k, n_exp))
    for k in range(1, TEAM):
        greet(first_member + lax.rem(spot + k, TEAM), side)

    @pl.when(row > 0)
    def _():
        greet(me - TEAM, side)

    @pl.when(row < teams - 1)
    def _():
        greet(me + TEAM, side)

    arrays = [
        (delta_any, delta_ref), (decay_any, decay_ref), (b_any, b_ref), (c_any, c_ref),
        (x_any, x_ref), (g_any, g_ref), (skip_any, skip_ref), (ids_any, ids_ref),
        (probs_any, probs_ref), (act_any, act_ref),
    ]
    loads = [
        pltpu.make_async_copy(src, dst, load_sem.at[i]) for i, (src, dst) in enumerate(arrays)
    ]
    for load in loads:
        load.start()
    experts, hidden = w_any.shape[0], w_any.shape[1]
    width = x_ref.shape[1]

    def w_load(e, owner):
        columns = pl.ds(pl.multiple_of(owner * width, width), width)
        return pltpu.make_async_copy(
            w_any.at[e, :, columns], w_ref.at[pl.ds(e * hidden, hidden)], load_w.at[e]
        )

    for e in range(experts):
        w_load(e, side).start()

    met = n_exp - 1 + TEAM - 1 + (row > 0).astype(jnp.int32) + (row < teams - 1).astype(jnp.int32)
    pl.semaphore_wait(barrier, met)

    length = x_ref.shape[0]
    sent = g_in.shape[3]
    sends = width // sent

    def to_partner(k, p):
        return pltpu.make_async_remote_copy(
            src_ref=g_any.at[:, pl.ds(p * sent, sent)],
            dst_ref=g_in.at[k - 1, p],
            send_sem=send_g.at[k - 1, p],
            recv_sem=recv_g.at[k - 1, p],
            device_id=(me, lax.rem(side + k, n_exp)),
            device_id_type=MESH,
        )

    for p in range(sends):
        for k in range(1, n_exp):
            to_partner(k, p).start()

    heads = delta_ref.shape[0]
    chunks = length // CHUNK
    parts = [slice(c * CHUNK, (c + 1) * CHUNK) for c in range(chunks)]
    pieces = width // PIECE
    per = LANES // HEAD_DIM
    held = PIECE // HEAD_DIM
    nstate = b_ref.shape[1]
    half = nstate // 2
    my_rows = pl.ds(pl.multiple_of(core * half, half), half)
    mate_rows = pl.ds(pl.multiple_of((1 - core) * half, half), half)

    def piece_lanes(p):
        return pl.ds(pl.multiple_of(p * PIECE, PIECE), PIECE)

    loads[0].wait()
    loads[1].wait()
    delta = delta_ref[...]
    rate_row = -jnp.exp(decay_ref[...])
    same = iota((heads, heads), 0) == iota((heads, heads), 1)
    rate = jnp.sum(jnp.where(same, rate_row, 0.0), axis=1, keepdims=True)
    upper = (iota((CHUNK, CHUNK), 0) <= iota((CHUNK, CHUNK), 1)).astype(BF16)
    pace = delta * rate
    rows = jnp.concatenate([pace[:, part] for part in parts], axis=0)
    sums = None
    for piece in split(rows, 3):
        term = nn(piece, upper)
        sums = term if sums is None else sums + term
    total = None
    for c in range(chunks):
        part = parts[c]
        log = sums[c * heads : (c + 1) * heads]
        end = log[:, CHUNK - 1 : CHUNK]
        total = end if total is None else total + end
        step = delta[:, part]
        lift_k[part] = stacked(jnp.exp(log)).T.astype(BF16)
        lift_k[length + c * CHUNK : length + (c + 1) * CHUNK] = (
            stacked(jnp.exp(end - log) * step).T.astype(BF16)
        )
        off_k[part] = stacked((jnp.log(step) - log) * LOG2E).T.astype(BF16)
        log = log * LOG2E
        for i in range(width // LANES):
            log_rows[i, :, part] = log[i * per : (i + 1) * per]
    through_row = jnp.sum(jnp.where(same, jnp.exp(total), 0.0), axis=0, keepdims=True)
    t_all[0] = jnp.broadcast_to(
        jnp.concatenate([through_row, jnp.zeros((1, LANES - heads), F32)], axis=1), (8, LANES)
    )

    def tell(k):
        return pltpu.make_async_remote_copy(
            src_ref=t_all.at[0],
            dst_ref=t_all.at[k],
            send_sem=send_t.at[k - 1],
            recv_sem=recv_t.at[k - 1],
            device_id=(first_member + lax.rem(spot + k, TEAM), side),
            device_id_type=MESH,
        )

    for k in range(1, TEAM):
        tell(k).start()

    stack_row = iota((3 * heads, PIECE), 0)
    stack_head = lax.rem(stack_row, heads)

    @pl.loop(0, pieces)
    def _(p):
        sel_ref[p] = (stack_head == p * held + iota((3 * heads, PIECE), 1) // HEAD_DIM).astype(BF16)

    loads[2].wait()
    loads[3].wait()
    b_two[...] = jnp.concatenate(split(b_ref[...], 2), axis=1)
    c_two[...] = jnp.concatenate(split(c_ref[...], 2), axis=1)
    b_t_ref[...] = b_ref[...].T.astype(BF16)
    c_t_ref[...] = c_ref[...].T.astype(BF16)
    loads[4].wait()
    loads[5].wait()

    def core_swap(d, k):
        return pltpu.make_async_remote_copy(
            src_ref=own.at[d, k, mate_rows],
            dst_ref=own_in.at[d, k],
            send_sem=send_c.at[d, k],
            recv_sem=recv_c.at[d, k],
            device_id=(mate, side),
            device_id_type=MESH,
        )

    def along(d, k):
        return pltpu.make_async_remote_copy(
            src_ref=z_out.at[d, k],
            dst_ref=z_in.at[d, k],
            send_sem=send_z.at[d, k],
            recv_sem=recv_z.at[d, k],
            device_id=(me + TEAM if d == 0 else me - TEAM, side),
            device_id_type=MESH,
        )

    def crossing(d, k):
        return pltpu.make_async_remote_copy(
            src_ref=x_out.at[d, k],
            dst_ref=x_in.at[d, k],
            send_sem=send_x.at[d, k],
            recv_sem=recv_x.at[d, k],
            device_id=(across, side),
            device_id_type=MESH,
        )

    def hand_over(d, k):
        return pltpu.make_async_remote_copy(
            src_ref=core_out.at[d, k],
            dst_ref=entry.at[d, k, my_rows],
            send_sem=send_d.at[d, k],
            recv_sem=recv_d.at[d, k],
            device_id=(mate, side),
            device_id_type=MESH,
        )

    leads = [core == 0, core == 1]
    near = [column == 0, column == 1]
    place = [row, teams - 1 - row]

    def own_unit(p):
        lanes = piece_lanes(p)
        sel = sel_ref[p]
        through, fwd, bwd = [], [], []
        lifted = nn(lift_k[...], sel)
        grow_x_ref[:, lanes] = lifted[:length]
        keep_x_ref[:, lanes] = lifted[length:]
        for c in range(chunks):
            part = parts[c]
            grow_x = lifted[part]
            keep_x = lifted[length + c * CHUNK : length + (c + 1) * CHUNK]
            kept = (x_ref[part, lanes].astype(F32) * keep_x).astype(BF16)
            grown = (g_ref[part, lanes].astype(F32) * grow_x).astype(BF16)
            kept_ref[part, lanes] = kept
            grown_ref[part, lanes] = grown
            through.append(grow_x[CHUNK - 1 : CHUNK, :])
            fwd.append(nn(b_t_ref[:, part], kept))
            bwd.append(nn(c_t_ref[:, part], grown))
            chunk_own[0, c, p] = fwd[c]
            chunk_own[1, c, p] = bwd[c]
        total_f, total_b = fwd[0], bwd[chunks - 1]
        for c in range(1, chunks):
            total_f = through[c] * total_f + fwd[c]
        for c in reversed(range(chunks - 1)):
            total_b = through[c] * total_b + bwd[c]
        own[0, p] = total_f
        own[1, p] = total_b
        core_swap(0, p).start()
        core_swap(1, p).start()

    def gather(k, d):
        lanes = piece_lanes(k)
        core_swap(d, k).wait_recv()
        mine, theirs = own[d, k, my_rows], own_in[d, k]
        first = jnp.where(leads[d], mine, theirs)
        second = jnp.where(leads[d], theirs, mine)
        pair_sum[d, k] = factor[d, 1, 0:1, lanes] * first + second

    def pass_on(k, d):
        lanes = piece_lanes(k)

        @pl.when(place[d] == 0)
        def _():
            z_in[d, k] = jnp.zeros((half, PIECE), BF16)

        @pl.when(place[d] > 0)
        def _():
            along(d, k).wait_recv()

        before, mine = z_in[d, k].astype(F32), pair_sum[d, k]

        @pl.when(place[d] < teams - 1)
        def _():
            sent_on = plane[0:1, lanes] * before + factor[d, 2, 0:1, lanes] * mine
            z_out[d, k] = sent_on.astype(BF16)
            along(d, k).start()

        x_out[d, k] = jnp.where(near[d], factor[d, 3, 0:1, lanes] * before + mine, before).astype(BF16)
        crossing(d, k).start()

    def settle(k, d):
        lanes = piece_lanes(k)
        crossing(d, k).wait_recv()
        before, other = z_in[d, k].astype(F32), x_in[d, k].astype(F32)
        into = jnp.where(near[d], before + other, factor[d, 3, 0:1, lanes] * before + other)
        first = jnp.where(leads[d], own[d, k, my_rows], own_in[d, k])
        after = factor[d, 0, 0:1, lanes] * into + first
        entry[d, k, my_rows] = jnp.where(leads[d], into, after)
        core_out[d, k] = jnp.where(leads[d], after, into)
        hand_over(d, k).start()

    def stage(step, offset, act, d):
        k = step - offset

        @pl.when((k >= 0) & (k < pieces))
        def _():
            act(k, d)

    def exchange(step):
        for d in range(2):
            stage(step, FIRST_LAP, gather, d)
            stage(step, FIRST_LAP + HOP_LAPS * place[d], pass_on, d)
            stage(step, FIRST_LAP + HOP_LAPS * place[d] + LAST_LAPS, settle, d)

    early = min(FIRST_LAP, pieces)
    for p in range(early):
        own_unit(p)

    for k in range(1, TEAM):
        tell(k).wait_recv()
    loads[6].wait()
    skip_row = jnp.broadcast_to(skip_ref[...], (8, heads))

    def over_lanes(value):
        return jnp.concatenate([part.astype(F32) for part in split(value, 3)], axis=1).astype(BF16)

    spread_rows = [over_lanes(t_all[k][:, :heads]) for k in range(TEAM)] + [over_lanes(skip_row)]
    spread_rows = jnp.concatenate([value.astype(F32) for value in spread_rows], axis=0).astype(BF16)

    @pl.loop(0, pieces)
    def _(p):
        lanes = piece_lanes(p)
        lifted = nn(spread_rows, sel_ref[p])
        for k in range(TEAM):
            t_lanes[k, :, lanes] = lifted[8 * k : 8 * k + 8]
        skip_x[:, lanes] = lifted[8 * TEAM : 8 * TEAM + 8]

    def through_of(member):
        return t_lanes[lax.rem(spot - member + TEAM, TEAM)]

    t0, t1, t2, t3 = [through_of(member) for member in range(TEAM)]
    pair0, pair1 = t0 * t1, t2 * t3
    low, high = jnp.where(column == 0, t0, t2), jnp.where(column == 0, t1, t3)
    plane[...] = pair0 * pair1
    factor[0, 0], factor[0, 1] = low, high
    factor[1, 0], factor[1, 1] = high, low
    factor[0, 2] = jnp.where(near[0], pair1, 1.0)
    factor[1, 2] = jnp.where(near[1], pair0, 1.0)
    factor[0, 3], factor[1, 3] = pair0, pair1

    @pl.loop(early, pieces)
    def _(p):
        own_unit(p)
        exchange(p)

    for load in loads[7:]:
        load.wait()
    for e in range(experts):
        w_load(e, side).wait()
    capacity = act_ref.shape[1]
    before = (iota((length, length), 0) < iota((length, length), 1)).astype(BF16)

    def pick_slots(e):
        named = ids_ref[...] == side * experts + e
        hit = jnp.sum(named.astype(F32), axis=0, keepdims=True)
        rank = nn(jnp.broadcast_to(hit, (16, length)).astype(BF16), before)[0:1, :]
        place_row = jnp.where(hit > 0.5, rank, -1.0)
        picked = iota((capacity, length), 0).astype(F32) == place_row
        chosen_ref[e] = picked.astype(BF16)
        prob = jnp.sum(jnp.where(named, probs_ref[...], 0.0), axis=0, keepdims=True)
        weight = jnp.sum(jnp.where(picked, prob, 0.0), axis=1, keepdims=True)
        weight_ref[e] = jnp.broadcast_to(weight, (capacity, LANES))

    blocks = product.shape[0]
    block = product.shape[2]
    joined = block // hidden

    def w_rows(i):
        return pl.ds(pl.multiple_of(i * block, block), block)

    @pl.loop(0, blocks)
    def _(i):
        for j in range(joined):
            pick_slots(i * joined + j)
        product[i] = nt(g_ref[...], w_ref[w_rows(i)])
        exchange(pieces + 2 * i)
        exchange(pieces + 2 * i + 1)

    def owner_of(k):
        return lax.rem(side + n_exp - k, n_exp)

    for e in range(experts):
        w_load(e, owner_of(1)).start()

    causal = iota((CHUNK, CHUNK), 1) >= iota((CHUNK, CHUNK), 0)
    for part in parts:
        gram_t[part] = jnp.where(causal, fine(nt, b_ref[part], c_ref[part]), 0.0)
    dgram_t[...] = jnp.zeros_like(dgram_t)
    pairs = width // LANES
    low_lanes = (iota((1, LANES), 1) < HEAD_DIM).astype(BF16)
    high_lanes = (iota((1, LANES), 1) >= HEAD_DIM).astype(BF16)
    wide_head = lax.rem(iota((3 * heads, per * CHUNK), 0), heads)

    def within_unit(i):
        lanes = pl.ds(pl.multiple_of(i * LANES, LANES), LANES)
        picks = (wide_head == i * per + iota((3 * heads, per * CHUNK), 1) // CHUNK).astype(BF16)
        offsets = nn(off_k[...], picks)
        for c in range(chunks):
            part = parts[c]
            g_part = g_ref[part, lanes]
            both = jnp.concatenate([g_part * low_lanes, g_part * high_lanes], axis=0)
            pair = nt(x_ref[part, lanes], both)
            offset = offsets[part]
            gram = gram_t[part]
            weighed = []
            total = None
            for j in range(per):
                columns = slice(j * CHUNK, (j + 1) * CHUNK)
                weight = jnp.exp2(offset[:, columns] + log_rows[i, j : j + 1, part])
                bent = weight * gram
                value = weight * pair[:, columns]
                total = value if total is None else total + value
                row_u[i, j : j + 1, part] = jnp.sum(bent * pair[:, columns], axis=0, keepdims=True)
                weighed.append(bent.astype(BF16))
            dgram_t[part] += total
            inside[part, lanes] = nn(jnp.concatenate(weighed, axis=1), both)

    turns = pairs // PAIRS

    @pl.loop(0, turns)
    def _(i):
        for j in range(PAIRS):
            within_unit(i * PAIRS + j)
        exchange(pieces + 2 * blocks + i)

    order = [(k, p) for k in range(1, n_exp) for p in range(sends)]
    groups = []
    for k in range(1, n_exp):
        mine = [p for p in range(sends) if (k, p) != order[-1]]
        groups += [(k, mine[i : i + 2]) for i in range(0, len(mine), 2)]

    def other_columns(k, group, act):
        if group[0] == 0:
            for e in range(experts):
                if k > 1:
                    w_load(e, owner_of(k)).start()
                w_load(e, owner_of(k)).wait()
        for p in group:
            to_partner(k, p).wait_recv()

        @pl.loop(0, blocks)
        def _(i):
            columns = slice(group[0] * sent, (group[-1] + 1) * sent)
            grads = jnp.concatenate([g_in[k - 1, p] for p in group], axis=1)
            product[i] += nt(grads, w_ref[w_rows(i), columns])
            act(i)

    base = pieces + 2 * blocks + turns
    ahead = groups[: len(groups) // 4]
    for n, (k, group) in enumerate(ahead):
        other_columns(k, group, lambda i, n=n: exchange(base + n * blocks + i))

    laps = base + len(ahead) * blocks
    needed = max(laps, FIRST_LAP + HOP_LAPS * (teams - 1) + LAST_LAPS + HAND_LAPS)

    if needed > laps:
        @pl.loop(laps, needed)
        def _(step):
            exchange(step)

    for part in parts:
        pull = jnp.where(causal, dgram_t[part], 0.0)
        part_b[part] = fine(nn, pull, c_ref[part])
        part_c[part] = fine(nn, pull.T, b_ref[part])
    end_ref[...] = jnp.zeros_like(end_ref)
    lane_head = lax.rem(iota((16, 4 * PIECE), 1), PIECE) // HEAD_DIM
    lane_kind = iota((16, 4 * PIECE), 1) // (2 * PIECE)
    gather_rows = (iota((16, 4 * PIECE), 0) == lane_head + held * lane_kind).astype(BF16)

    def across_unit(p):
        lanes = piece_lanes(p)
        hand_over(0, p).wait_recv()
        hand_over(1, p).wait_recv()
        through = [grow_x_ref[(c + 1) * CHUNK - 1 : (c + 1) * CHUNK, lanes] for c in range(chunks)]
        states = [entry[0, p]]
        for c in range(chunks):
            states.append(through[c] * states[c] + chunk_own[0, c, p])
        grads = [None] * chunks + [entry[1, p]]
        for c in reversed(range(1, chunks)):
            grads[c] = through[c] * grads[c + 1] + chunk_own[1, c, p]
        skip = skip_x[0:1, lanes]
        for c in range(chunks):
            part = parts[c]
            state, grad = states[c].astype(BF16), grads[c + 1].astype(BF16)
            x_part, g_part = x_ref[part, lanes].astype(F32), g_ref[part, lanes].astype(F32)
            keep_x, grow_x = keep_x_ref[part, lanes], grow_x_ref[part, lanes]
            from_grad = nn(b_two[part], jnp.concatenate([grad, grad], axis=0)) * keep_x
            from_state = nn(c_two[part], jnp.concatenate([state, state], axis=0)) * grow_x
            kept, grown = kept_ref[part, lanes], grown_ref[part, lanes]
            kept_two = jnp.concatenate([kept, (x_part * keep_x - kept.astype(F32)).astype(BF16)], axis=1)
            grown_two = jnp.concatenate([grown, (g_part * grow_x - grown.astype(F32)).astype(BF16)], axis=1)
            part_c[part] += nt(grown_two, jnp.concatenate([state, state], axis=1))
            part_b[part] += nt(kept_two, jnp.concatenate([grad, grad], axis=1))
            inner = inside[part, lanes] + from_grad
            grad_x_ref[part, lanes] = (inner + skip * g_part).astype(BF16)
            end_ref[c : c + 1, lanes] = jnp.sum(states[c + 1] * grads[c + 1], axis=0, keepdims=True)
            summed = split(x_part * inner, 2) + split(g_part * from_state, 2)
            uv_ref[p, :, part] = nt(gather_rows, jnp.concatenate(summed, axis=1))

    def grad_x_out(p):
        lanes = piece_lanes(p)
        return pltpu.make_async_copy(grad_x_ref.at[:, lanes], grad_x_any.at[:, lanes], save_x.at[p])

    @pl.loop(0, pieces)
    def _(p):
        exchange(needed + p)
        across_unit(p)
        grad_x_out(p).start()

    share = grad_b_ref.shape[0]

    def shed(k, source, landing, send, recv):
        target = lax.rem(side + k, n_exp)
        return pltpu.make_async_remote_copy(
            src_ref=source.at[pl.ds(pl.multiple_of(target * share, share), share)],
            dst_ref=landing.at[k - 1],
            send_sem=send.at[k - 1],
            recv_sem=recv.at[k - 1],
            device_id=(me, target),
            device_id_type=MESH,
        )

    out_b[...] = part_b[...].astype(BF16)
    out_c[...] = part_c[...].astype(BF16)
    for k in range(1, n_exp):
        shed(k, out_b, land_b, send_p, recv_p).start()
        shed(k, out_c, land_c, send_q, recv_q).start()

    endings = None
    for piece in split(end_ref[...], 2):
        term = None
        for p in range(pieces):
            value = nt(piece[:, p * PIECE : (p + 1) * PIECE], sel_ref[p, 0:heads])
            term = value if term is None else term + value
        endings = term if endings is None else endings + term
    endings = endings.T
    v_rows = jnp.concatenate([uv_ref[p, 0:held] for p in range(pieces)], axis=0)
    u_rows = jnp.concatenate([uv_ref[p, held : 2 * held] for p in range(pieces)], axis=0)
    net = jnp.concatenate([row_u[i] for i in range(pairs)], axis=0) + u_rows - v_rows
    lower = (iota((CHUNK, CHUNK), 0) >= iota((CHUNK, CHUNK), 1)).astype(BF16)
    rows = jnp.concatenate([net[:, part] for part in parts], axis=0)
    sums = None
    for piece in split(rows, 3):
        term = nn(piece, lower)
        sums = term if sums is None else sums + term
    for c in range(chunks):
        part = parts[c]
        drift = sums[c * heads : (c + 1) * heads] + endings[:, c : c + 1]
        grad_delta_ref[:, part] = v_rows[:, part] / delta_ref[:, part] + rate * drift

    grad_delta_out = pltpu.make_async_copy(grad_delta_ref, grad_delta_any, save_sem.at[0])
    grad_delta_out.start()

    for k, group in groups[len(ahead) :]:
        other_columns(k, group, lambda i: None)
    for e in range(experts):
        total = None
        hidden_columns = slice((e % joined) * hidden, (e % joined + 1) * hidden)
        for piece in split(product[e // joined, :, hidden_columns], 2):
            term = nn(chosen_ref[e], piece)
            total = term if total is None else total + term
        act_sum[e] = total
    mine = pl.ds(pl.multiple_of(side * share, share), share)
    total_b, total_c = part_b[mine], part_c[mine]
    for k in range(1, n_exp):
        shed(k, out_b, land_b, send_p, recv_p).wait_recv()
        shed(k, out_c, land_c, send_q, recv_q).wait_recv()
        total_b = total_b + land_b[k - 1].astype(F32)
        total_c = total_c + land_c[k - 1].astype(F32)
    grad_b_ref[...] = total_b
    grad_c_ref[...] = total_c
    sums_out = [
        pltpu.make_async_copy(grad_b_ref, grad_b_any, save_sem.at[1]),
        pltpu.make_async_copy(grad_c_ref, grad_c_any, save_sem.at[2]),
    ]
    for copy in sums_out:
        copy.start()
    slots_out = pltpu.make_async_copy(grad_slots_ref, grad_slots_any, save_sem.at[3])
    k, p = order[-1]
    to_partner(k, p).wait_recv()
    act_out = [
        pltpu.make_async_copy(grad_act_ref.at[e], grad_act_any.at[e], save_act.at[e])
        for e in range(experts)
    ]
    for e in range(experts):
        taken = nn(chosen_ref[e], g_in[k - 1, p]).astype(BF16)
        inner = act_sum[e] + nt(taken, w_ref[e * hidden : (e + 1) * hidden, p * sent : (p + 1) * sent])
        grad_act_ref[e] = (weight_ref[e][:, 0:1] * inner).astype(BF16)
        act_out[e].start()
        scored = act_ref[e].astype(F32) * inner
        ones = jnp.ones((16, scored.shape[1]), BF16)
        summed = None
        for piece in split(scored, 2):
            term = nt(ones, piece)
            summed = term if summed is None else summed + term
        grad_slots_ref[e : e + 1, :] = summed[0:1, :]

    slots_out.start()
    last = sums_out + [slots_out]

    for k in range(1, n_exp):
        shed(k, out_b, land_b, send_p, recv_p).wait_send()
        shed(k, out_c, land_c, send_q, recv_q).wait_send()
        for p in range(sends):
            to_partner(k, p).wait_send()
    for k in range(1, TEAM):
        tell(k).wait_send()

    @pl.loop(0, pieces)
    def _(p):
        grad_x_out(p).wait()
        for d in range(2):
            core_swap(d, p).wait_send()
            crossing(d, p).wait_send()
            hand_over(d, p).wait_send()

            @pl.when(place[d] < teams - 1)
            def _():
                along(d, p).wait_send()

    for copy in act_out + [grad_delta_out] + last:
        copy.wait()


def store_kernel(count, *refs):
    sources, targets, held = refs[:count], refs[count : 2 * count], refs[2 * count : 3 * count]
    load_sem, save_sem = refs[3 * count :]
    pairs = []
    for source, target, buffer in zip(sources, targets, held):
        rows = source.shape[0]
        cut = rows // STORE_CUTS if rows % (8 * STORE_CUTS) == 0 and source.dtype == BF16 else rows
        for start in range(0, rows, cut):
            pairs.append([ref.at[start : start + cut] for ref in (source, buffer, target)])
    loads = [pltpu.make_async_copy(a, b, load_sem.at[i]) for i, (a, b, _) in enumerate(pairs)]
    saves = [pltpu.make_async_copy(b, c, save_sem.at[i]) for i, (_, b, c) in enumerate(pairs)]
    for load in loads:
        load.start()
    for load, save in zip(loads, saves):
        load.wait()
        save.start()
    for save in saves:
        save.wait()


def per_device(
    n_ctx, n_exp,
    feature_in, grad_out, delta, decay_log, skip_gain, b_proj, c_proj,
    route_ids, route_probs, w_down, saved_act,
):
    length, width = feature_in.shape
    heads = delta.shape[0]
    nstate = b_proj.shape[1]
    experts, hidden, full = w_down.shape
    capacity = saved_act.shape[2]
    topk = route_ids.shape[1]
    share = length // n_exp
    others = n_exp - 1
    chunks = length // CHUNK
    pieces = width // PIECE
    half = nstate // 2
    sent = min(SENT, width)
    sends = width // sent
    joined = 2 - experts % 2
    hbm = pl.BlockSpec(memory_space=pltpu.HBM)
    dma = pltpu.SemaphoreType.DMA
    inputs = (
        feature_in, grad_out, delta, decay_log[None, :], skip_gain[None, :], b_proj, c_proj,
        route_ids.T, route_probs.T, saved_act[0], w_down,
    )
    shard = jax.ShapeDtypeStruct((share, nstate), F32)
    shapes = (
        jax.ShapeDtypeStruct((length, width), BF16),
        jax.ShapeDtypeStruct((heads, length), F32),
        shard,
        shard,
        jax.ShapeDtypeStruct((experts, capacity, hidden), BF16),
        jax.ShapeDtypeStruct((experts, capacity), F32),
    )
    by_state = pltpu.VMEM((length, nstate), F32)
    per = LANES // HEAD_DIM
    by_pair = pltpu.VMEM((heads // per, per, length), F32)
    wide = pltpu.VMEM((length, width), F32)
    narrow = pltpu.VMEM((length, width), BF16)
    halves = pltpu.VMEM((2, pieces, half, PIECE), F32)
    halves_bf = pltpu.VMEM((2, pieces, half, PIECE), BF16)
    whole = pltpu.VMEM((2, pieces, nstate, PIECE), F32)
    results = pl.pallas_call(
        partial(block_kernel, n_ctx, n_exp),
        out_shape=shapes,
        in_specs=[hbm] * len(inputs),
        out_specs=(hbm,) * len(shapes),
        scratch_shapes=[pltpu.VMEM(value.shape, value.dtype) for value in shapes + inputs[:-1]]
        + [pltpu.VMEM((experts * hidden, width), BF16)]
        + [
            pltpu.VMEM((others, sends, length, sent), BF16),
            pltpu.VMEM((TEAM, 8, LANES), F32),
            pltpu.VMEM((TEAM, 8, width), F32),
            pltpu.VMEM((2, 4, 8, width), F32),
            pltpu.VMEM((8, width), F32),
            pltpu.VMEM((8, width), F32),
            pltpu.VMEM((pieces, 3 * heads, PIECE), BF16),
        ]
        + [pltpu.VMEM((2 * length, 3 * heads), BF16), pltpu.VMEM((length, 3 * heads), BF16)]
        + [by_pair]
        + [pltpu.VMEM((length, 2 * nstate), BF16)] * 2
        + [pltpu.VMEM((nstate, length), BF16)] * 2
        + [pltpu.VMEM((length, CHUNK), F32)] * 2
        + [by_pair]
        + [pltpu.VMEM((pieces, 16, length), F32), pltpu.VMEM((8, width), F32)]
        + [by_state] * 2
        + [pltpu.VMEM((length, nstate), BF16)] * 2
        + [pltpu.VMEM((others, share, nstate), BF16)] * 2
        + [pltpu.VMEM((2, chunks, pieces, nstate, PIECE), F32)]
        + [whole]
        + [halves] * 2
        + [halves_bf] * 4
        + [halves, whole]
        + [wide] * 2
        + [narrow] * 2
        + [wide]
        + [
            pltpu.VMEM((experts // joined, length, joined * hidden), F32),
            pltpu.VMEM((experts, capacity, hidden), F32),
            pltpu.VMEM((experts, capacity, length), BF16),
            pltpu.VMEM((experts, capacity, LANES), F32),
        ]
        + [dma((10,)), dma((experts,)), dma((pieces,)), dma((experts,)), dma((4,))]
        + [dma((others, sends))] * 2
        + [dma((TEAM - 1,))] * 2
        + [dma((2, pieces))] * 8
        + [dma((others,))] * 4,
        compiler_params=pltpu.CompilerParams(
            collective_id=0, has_side_effects=True, vmem_limit_bytes=60 << 20
        ),
        name="block_grads",
    )(*inputs)
    grad_x, grad_delta, grad_b, grad_c, grad_act, grad_slots = pl.pallas_call(
        partial(store_kernel, len(shapes)),
        out_shape=shapes,
        in_specs=[hbm] * len(shapes),
        out_specs=(hbm,) * len(shapes),
        scratch_shapes=[pltpu.VMEM(value.shape, value.dtype) for value in shapes]
        + [dma((len(shapes) + STORE_CUTS,))] * 2,
        compiler_params=pltpu.CompilerParams(vmem_limit_bytes=60 << 20),
        name="store",
    )(*results)
    return (grad_x, grad_delta, grad_b, grad_c, grad_act[None], grad_slots[None])


def solution(mesh):
    placed = (
        P("ctx", "exp"),
        P("ctx", "exp"),
        P("exp", "ctx"),
        P("exp"),
        P("exp"),
        P("ctx", None),
        P("ctx", None),
        P("ctx", None),
        P("ctx", None),
        P("exp", None, None),
        P("ctx", "exp", None, None),
    )
    return jax.shard_map(
        partial(per_device, mesh.shape["ctx"], mesh.shape["exp"]),
        mesh=mesh,
        in_specs=placed,
        out_specs=(
            P("ctx", "exp"),
            P("exp", "ctx"),
            P(("ctx", "exp"), None),
            P(("ctx", "exp"), None),
            P("ctx", "exp", None, None),
            P("ctx", "exp", None),
        ),
        check_vma=False,
    )
```
